32 devices in a mesh: groups: 2 (over y), fsdp: 4 (over z), rep: 4 (over x, core).
Axes of the slice: x: 2, y: 2, z: 4, core: 2. Of those that a mesh axis runs over, the one named last changes fastest.
Arguments:
- images: bfloat16 [8, 16, 256, 320], P(('groups', 'rep'), 'fsdp'), parts along dimension 0, may hold values from -60 to 60
- gains: float32 [2, 320], replicated, may hold values from 0.5 to 1.5
- conv_weight: bfloat16 [2880, 320], P('fsdp'), may hold values from -0.109375 to 0.109375
- cotangent: bfloat16 [8, 8, 128, 320], P(('groups', 'rep'), 'fsdp'), parts along dimension 0, may hold values from -60 to 60
Outputs:
- output_maps: bfloat16 [8, 8, 128, 320], P(('groups', 'rep'), 'fsdp'), parts along dimension 0
- input_grad: bfloat16 [8, 16, 256, 320], P(('groups', 'rep'), 'fsdp'), parts along dimension 0
- weight_grad: float32 [5760, 320], P(('groups', 'fsdp')), parts along dimension 0
- gain_grad: float32 [4, 320], P('groups'), parts along dimension 0
The draws below stay inside these ranges and needn't reach their ends.
There are 2 independent parts, one for each index of `groups`. The reference program is written for one: setup_inputs(seed, part) draws one part's arguments, and reference() takes and returns one part's arrays. A program takes and returns all parts, laid end to end along the dimension named above; an argument that names none is the same for every part. Nothing has to cross between parts.
All inputs are finite; a program needn't handle non-finite values.
Results may differ from the reference program's by a relative error of at most 0.0095.
Values may be sent and summed in bfloat16 or wider, within the bound.
A program may use at most 64 MiB of HBM per device.

```python
import math
import jax
import jax.numpy as jnp
from jax import lax

W = 256
C = 320
CO = 320
GROUPS = 32
BATCH = 4
H = 16
HO = 8
WO = 128


def rough_field(key, batch, rows, cols, chans, offset):
    keys = jax.random.split(key, 4)
    position = jnp.arange(rows, dtype=jnp.float32) / rows
    row_scale = jnp.exp(position * math.log(3.0) + jax.random.uniform(keys[0], (rows,), jnp.float32, 0.0, math.log(3.3)))
    chan_scale = jnp.exp(jax.random.uniform(keys[1], (chans,), jnp.float32, math.log(0.5), math.log(2.0)))
    chan_mean = offset * jax.random.uniform(keys[2], (chans,), jnp.float32, -1.0, 1.0)
    noise = jax.random.normal(keys[3], (batch, rows, cols, chans), jnp.float32)
    field = (chan_mean + chan_scale * noise) * row_scale[None, :, None, None]
    return jnp.clip(field, -60.0, 60.0)


def draw_images(key, part):
    return rough_field(jax.random.fold_in(key, 11), BATCH, H, W, C, 1.0).astype(jnp.bfloat16)


def draw_cotangent(key, part):
    return rough_field(jax.random.fold_in(key, 23), BATCH, HO, WO, CO, 0.0).astype(jnp.bfloat16)


def block_scale(rng, dims, cuts, least, largest):
    loudness = 1.0
    for dim, shards_of in cuts:
        heights = jax.random.uniform(jax.random.fold_in(jax.random.fold_in(rng, 6), dim), (shards_of,), jnp.float32, least / len(cuts), largest / len(cuts))
        loudness = loudness * jnp.repeat(jnp.exp(heights), dims[dim] // shards_of).reshape((-1,) + (1,) * (len(dims) - 1 - dim))
    return loudness


def centred(key, shape, spread, limit, cuts=(), kind=jnp.bfloat16):
    drawn = jax.random.normal(key, shape, jnp.float32) * spread
    if len(cuts) > 0:
        drawn = block_scale(key, shape, cuts, -0.22, 0.18) * drawn
    return jnp.clip(drawn, min=-limit, max=limit).astype(kind)


def setup_inputs(seed: int = 0, part: int = 0) -> dict:
    key_list = jax.random.split(jax.random.key(seed), 5)
    part_keys = jax.random.split(jax.random.fold_in(key_list[4], part), 5)
    return {
        "images": draw_images(jax.random.fold_in(jax.random.fold_in(key_list[4], part), 71), part),
        "gains": jnp.clip(jax.random.uniform(key_list[1], (2, C), jnp.float32, 0.5, 1.5), 0.5, 1.5),
        "conv_weight": centred(key_list[2], (9 * C, CO), (9 * C) ** -0.5, 0.109375, ((0, 4),)),
        "cotangent": draw_cotangent(jax.random.fold_in(jax.random.fold_in(key_list[4], part), 71), part),
    }


def conv_full(act, kernel):
    return lax.conv_general_dilated(act, kernel, (2, 2), ((1, 1), (1, 1)), dimension_numbers=('NHWC', 'HWIO', 'NHWC'), precision=lax.Precision.HIGHEST)

def one_image(gains, kernel, pair):
    image, grad_out = pair
    x = image.astype(jnp.float32)[None]
    rows, cols, chans = (x.shape[1], x.shape[2], x.shape[3])
    per_group = chans // GROUPS
    count = rows * cols * per_group
    grouped = x.reshape(1, rows, cols, GROUPS, per_group)
    mean = lax.optimization_barrier(jnp.sum(grouped, axis=(1, 2, 4))) / count
    meansq = lax.optimization_barrier(jnp.sum(grouped * grouped, axis=(1, 2, 4))) / count
    rstd = 1.0 / jnp.sqrt(meansq - mean * mean + 1e-05)
    normed = ((grouped - mean[:, None, None, :, None]) * rstd[:, None, None, :, None]).reshape(x.shape)
    z_val = gains[0] * normed + gains[1]
    act = (z_val * jax.nn.sigmoid(z_val)).astype(jnp.bfloat16)
    result, pullback = jax.vjp(conv_full, act.astype(jnp.float32), kernel)
    act_grad, kernel_grad = pullback(grad_out.astype(jnp.float32)[None])
    sig = jax.nn.sigmoid(z_val)
    z_grad = act_grad * sig * (1.0 + z_val * (1.0 - sig))
    u_sum = lax.optimization_barrier(jnp.sum(z_grad * normed, axis=(1, 2)))
    v_sum = lax.optimization_barrier(jnp.sum(z_grad, axis=(1, 2)))
    su_val = lax.optimization_barrier(jnp.sum((gains[0] * u_sum).reshape(1, GROUPS, per_group), axis=-1))
    sv_val = lax.optimization_barrier(jnp.sum((gains[0] * v_sum).reshape(1, GROUPS, per_group), axis=-1))
    scaled = (gains[0] * z_grad).reshape(grouped.shape)
    normed_g = normed.reshape(grouped.shape)
    dx_val = rstd[:, None, None, :, None] * (scaled - sv_val[:, None, None, :, None] / count - normed_g * su_val[:, None, None, :, None] / count)
    input_grad = dx_val.reshape(x.shape)[0].astype(jnp.bfloat16)
    return (result[0].astype(jnp.bfloat16), input_grad, kernel_grad, jnp.stack([u_sum[0], v_sum[0]]))

def reference(images, gains, conv_weight, cotangent):
    chans = images.shape[3]
    outs_ch = conv_weight.shape[1]
    kernel = conv_weight.astype(jnp.float32).reshape(3, 3, chans, outs_ch)
    output_maps, input_grad, kernel_grads, gain_parts = lax.map(lambda pair: one_image(gains, kernel, pair), (images, cotangent))
    scale = 1.0 / jnp.sqrt(jnp.float32(BATCH * HO * WO))
    weight_grad = lax.optimization_barrier(jnp.sum(kernel_grads, axis=0)).reshape(9 * chans, outs_ch) * scale
    gain_grad = lax.optimization_barrier(jnp.sum(gain_parts, axis=0)) * scale
    return (output_maps, input_grad, weight_grad, gain_grad)
```

```python
import functools

import jax
import jax.numpy as jnp
from jax import lax
from jax.experimental import pallas as pl
from jax.experimental.pallas import tpu as pltpu
from jax.sharding import PartitionSpec as P

GROUPS = 32
MESH = pl.DeviceIdType.MESH


def passed_along(shard, axis, by):
    size = lax.axis_size(axis)
    pairs = [(i, i + by) for i in range(size) if 0 <= i + by < size]
    return lax.ppermute(shard, axis, pairs)


def spread_taps(first, middle, last, axis):
    length = first.shape[axis]
    widths_end = [(0, 0)] * first.ndim
    widths_end[axis] = (0, 1)
    widths_start = [(0, 0)] * first.ndim
    widths_start[axis] = (1, 0)
    even = jnp.pad(first, widths_end) + jnp.pad(last, widths_start)
    odd = jnp.pad(middle, widths_end)
    merged = jnp.stack([even, odd], axis=axis + 1)
    shape = list(even.shape)
    shape[axis] = 2 * (length + 1)
    merged = merged.reshape(shape)
    return lax.slice_in_dim(merged, 0, 2 * length + 1, axis=axis)


def shards(images, gains, conv_weight, cotangent):
    batch, rows, width, chans = images.shape
    outs_ch = conv_weight.shape[1]
    n_fsdp = lax.axis_size("fsdp")
    per_group = chans // GROUPS
    x_val = images.astype(jnp.float32)
    grouped = x_val.reshape(batch, rows, width, GROUPS, per_group)
    part_one = jnp.sum(grouped, axis=(1, 2, 4))
    part_two = jnp.sum(grouped * grouped, axis=(1, 2, 4))
    full_weight = lax.all_gather(conv_weight, "fsdp", axis=0, tiled=True)
    sum_one, sum_two = lax.psum((part_one, part_two), "fsdp")
    count = rows * n_fsdp * width * per_group
    mean = sum_one / count
    rstd = 1.0 / jnp.sqrt(sum_two / count - mean * mean + 1e-05)
    normed_g = (grouped - mean[:, None, None, :, None]) * rstd[:, None, None, :, None]
    normed = normed_g.reshape(x_val.shape)
    z_val = gains[0] * normed + gains[1]
    act = (z_val * jax.nn.sigmoid(z_val)).astype(jnp.bfloat16)
    above = passed_along(act[:, rows - 1 : rows], "fsdp", 1)
    padded = jnp.concatenate([above, act], axis=1)
    kernel = full_weight.reshape(3, 3, chans, outs_ch)
    result = lax.conv_general_dilated(
        padded,
        kernel,
        (2, 2),
        ((0, 0), (1, 0)),
        dimension_numbers=("NHWC", "HWIO", "NHWC"),
        preferred_element_type=jnp.float32,
    )
    output_maps = result.astype(jnp.bfloat16)
    patch_grad = jnp.einsum(
        "bijo,ko->bijk", cotangent, full_weight, preferred_element_type=jnp.float32
    )
    half_rows, half_cols = (cotangent.shape[1], cotangent.shape[2])
    taps = patch_grad.reshape(batch, half_rows, half_cols, 3, 3, chans)
    by_row = [
        spread_taps(
            taps[:, :, :, row_tap, 0], taps[:, :, :, row_tap, 1], taps[:, :, :, row_tap, 2], 2
        )
        for row_tap in range(3)
    ]
    grid = spread_taps(by_row[0], by_row[1], by_row[2], 1)[:, :, 1:]
    from_below = passed_along(grid[:, 0:1].astype(jnp.bfloat16), "fsdp", -1).astype(jnp.float32)
    filler = jnp.zeros((batch, rows - 1, width, chans), jnp.float32)
    act_grad = grid[:, 1:] + jnp.concatenate([filler, from_below], axis=1)
    padded_cols = jnp.pad(padded, ((0, 0), (0, 0), (1, 0), (0, 0)))
    blocks = []
    for row_tap in range(3):
        for col_tap in range(3):
            window = padded_cols[:, row_tap : row_tap + rows : 2, col_tap : col_tap + width : 2]
            blocks.append(
                jnp.einsum("bijc,bijo->co", window, cotangent, preferred_element_type=jnp.float32)
            )
    total_pixels = batch * lax.axis_size("rep") * half_rows * n_fsdp * half_cols
    scale = 1.0 / jnp.sqrt(jnp.float32(total_pixels))
    weight_term = jnp.concatenate(blocks, axis=0) * scale
    sig = jax.nn.sigmoid(z_val)
    z_grad = act_grad * sig * (1.0 + z_val * (1.0 - sig))
    u_part = jnp.sum(z_grad * normed, axis=(1, 2))
    v_part = jnp.sum(z_grad, axis=(1, 2))
    u_sum, v_sum = lax.psum((u_part, v_part), "fsdp")
    gain_term = jnp.stack([jnp.sum(u_sum, axis=0), jnp.sum(v_sum, axis=0)]) * scale
    su_val = jnp.sum((gains[0] * u_sum).reshape(batch, GROUPS, per_group), axis=-1)
    sv_val = jnp.sum((gains[0] * v_sum).reshape(batch, GROUPS, per_group), axis=-1)
    scaled = (gains[0] * z_grad).reshape(grouped.shape)
    dx_val = rstd[:, None, None, :, None] * (
        scaled
        - sv_val[:, None, None, :, None] / count
        - normed_g * su_val[:, None, None, :, None] / count
    )
    input_grad = dx_val.reshape(x_val.shape).astype(jnp.bfloat16)
    owned = lax.psum_scatter(weight_term, "fsdp", scatter_dimension=0, tiled=True)
    weight_grad, gain_grad = (
        lax.psum(owned.astype(jnp.bfloat16), "rep").astype(jnp.float32),
        lax.psum(gain_term.astype(jnp.bfloat16), "rep").astype(jnp.float32),
    )
    return (output_maps, input_grad, weight_grad, gain_grad)


ROW_SLOT = (0, 3, 1, 4, 2)
TAP_OFF = (0, 3, 1)


def dot(lhs, rhs, contract=((1,), (0,)), precision=None):
    return lax.dot_general(
        lhs, rhs, (contract, ((), ())), precision=precision, preferred_element_type=jnp.float32
    )


def fused(
    nz,
    x_ref,
    g_ref,
    w_ref,
    ct_ref,
    out_ref,
    dx_ref,
    wg_ref,
    gg_ref,
    xh,
    cth,
    norm,
    dsilu,
    zgrad,
    acts,
    cts,
    css,
    wfull,
    stat,
    stat_in,
    part,
    core_in,
    half,
    x_in,
    quarter,
    z_in,
    final,
    rep_in,
    uv,
    uv_in,
    uvt,
    uvt_in,
    halo_sem,
    stat_sem,
    w_sem,
    tail_sem,
    core_sem,
    x_sem,
    z_sem,
    rep_sem,
    uv_sem,
    uvt_sem,
    loc_sem,
):
    f32, bf16 = jnp.float32, jnp.bfloat16
    rows, width, chans = x_ref.shape[1:]
    cols = width // 2
    block = w_ref.shape[0]
    quart = quarter.shape[1]
    step = (block - quart) // 3
    count = rows * nz * width * (chans // GROUPS)
    scale = 1.0 / jnp.sqrt(f32(4 * nz * ct_ref.shape[1] * cols))
    z = lax.axis_index("fsdp")
    rep = lax.axis_index("rep")
    xi, ci = rep // 2, rep % 2
    mine = 2 * ci + xi
    peers_z = [lax.rem(z + d, nz) for d in range(1, nz)]
    reps = [(2 * xi + 1 - ci), (2 * (1 - xi) + ci), (2 * (1 - xi) + 1 - ci)]
    core_peer, x_peer = reps[0], reps[1]

    def aligned(value):
        return pl.multiple_of(value, 16)

    def remote(src, dst, sem, device):
        return pltpu.make_async_remote_copy(
            src_ref=src,
            dst_ref=dst,
            send_sem=sem.at[0],
            recv_sem=sem.at[1],
            device_id=device,
            device_id_type=MESH,
        )

    barrier = pltpu.get_barrier_semaphore()
    for peer in peers_z:
        pl.semaphore_signal(barrier, inc=1, device_id={"fsdp": peer}, device_id_type=MESH)
    for peer in reps:
        pl.semaphore_signal(barrier, inc=1, device_id={"rep": peer}, device_id_type=MESH)

    own_w = pltpu.make_async_copy(w_ref, wfull.at[pl.ds(aligned(z * block), block)], loc_sem.at[0])
    own_w.start()

    big_i = lax.broadcasted_iota(jnp.int32, (width, width), 0)
    big_j = lax.broadcasted_iota(jnp.int32, (width, width), 1)
    split = jnp.where(
        jnp.where(big_i < cols, 2 * big_i, 2 * (big_i - cols) + 1) == big_j, 1.0, 0.0
    ).astype(bf16)
    merge = jnp.where(
        jnp.where(big_j < cols, 2 * big_j, 2 * (big_j - cols) + 1) == big_i, 1.0, 0.0
    ).astype(bf16)
    inv = 1.0 / (chans // GROUPS)
    grp_i = jnp.floor((lax.broadcasted_iota(jnp.int32, (chans, chans), 0).astype(f32) + 0.5) * inv)
    grp_j = jnp.floor((lax.broadcasted_iota(jnp.int32, (chans, chans), 1).astype(f32) + 0.5) * inv)
    same = jnp.where(grp_i == grp_j, 1.0, 0.0)

    sum_one = jnp.zeros((1, chans), f32)
    sum_two = jnp.zeros((1, chans), f32)
    for r in range(rows):
        x_val = dot(split, x_ref[0, r])
        norm[r + 1] = x_val
        sum_one = sum_one + jnp.sum(x_val, axis=0, keepdims=True)
        sum_two = sum_two + jnp.sum(x_val * x_val, axis=0, keepdims=True)
    stat[...] = jnp.zeros(stat.shape, f32)
    stat[0:1] = sum_one
    stat[1:2] = sum_two

    pl.semaphore_wait(barrier, nz - 1 + 3)

    stat_cp = [
        remote(stat, stat_in.at[d], stat_sem.at[d], {"fsdp": peers_z[d]}) for d in range(nz - 1)
    ]
    for cp in stat_cp:
        cp.start()

    halo_x = remote(x_ref.at[0, rows - 1], xh, halo_sem.at[0], {"fsdp": lax.rem(z + 1, nz)})
    halo_c = remote(ct_ref.at[0, 0], cth, halo_sem.at[1], {"fsdp": lax.rem(z + nz - 1, nz)})

    @pl.when(z < nz - 1)
    def _():
        halo_x.start()

    @pl.when(z > 0)
    def _():
        halo_c.start()

    my_off = step * mine
    piece = aligned(z * block + my_off)
    w_cp, tail_cp = [], []
    for d in range(nz - 1):
        w_cp.append(
            remote(
                w_ref.at[pl.ds(aligned(my_off), step)],
                wfull.at[pl.ds(piece, step)],
                w_sem.at[0, d],
                {"fsdp": peers_z[d]},
            )
        )
        tail = block - 4 * step
        tail_cp.append(
            remote(
                w_ref.at[pl.ds(4 * step, tail)],
                wfull.at[pl.ds(aligned(z * block + 4 * step), tail)],
                tail_sem.at[d],
                {"fsdp": peers_z[d]},
            )
        )
    for d in range(nz - 1):
        w_cp[d].start()
        tail_cp[d].start()

    row_id = lax.broadcasted_iota(jnp.int32, (cols, chans), 0)

    @pl.when(z == nz - 1)
    def _():
        cth[...] = jnp.zeros(cth.shape, bf16)

    @pl.when(z == 0)
    def _():
        xh[...] = jnp.zeros(xh.shape, bf16)

    @pl.when(z < nz - 1)
    def _():
        halo_c.wait_recv()

    for i in range(3):
        value = ct_ref[0, i] if i < 2 else cth[...]
        cts[i * cols : (i + 1) * cols] = value
        moved = pltpu.roll(value.astype(f32), cols - 1, axis=0)
        css[i * cols : (i + 1) * cols] = jnp.where(row_id == cols - 1, 0.0, moved).astype(bf16)

    for cp in stat_cp:
        cp.wait_recv()
    total = stat[...]
    for d in range(nz - 1):
        total = total + stat_in[d]
    total = dot(total, same, precision=lax.Precision.HIGHEST)
    mean = total[0:1] / count
    rstd = 1.0 / jnp.sqrt(total[1:2] / count - mean * mean + 1e-05)
    gain = g_ref[0:1]
    shift = g_ref[1:2]

    for r in (1, 2, 3, 4, 0):
        if r == 0:

            @pl.when(z > 0)
            def _():
                halo_x.wait_recv()

            norm[0] = dot(split, xh[...])
        slot = ROW_SLOT[r]
        here = pl.ds(slot * cols, cols)
        for odd in range(2):
            part_rows = pl.ds(odd * cols, cols)
            normed = (norm[r, part_rows] - mean) * rstd
            z_val = gain * normed + shift
            sig = 0.5 * jnp.tanh(0.5 * z_val) + 0.5
            act = z_val * sig
            if r == 0:
                act = act * jnp.where(z > 0, 1.0, 0.0)
            else:
                norm[r, part_rows] = normed
                dsilu[r - 1, part_rows] = sig * (1.0 + z_val * (1.0 - sig))
            acts[1 + odd, here] = act.astype(bf16)
            if odd == 1:
                moved = pltpu.roll(act, 1, axis=0)
                acts[0, here] = jnp.where(row_id == 0, 0.0, moved).astype(bf16)

    grad_rows = cts[0 : 2 * cols]
    for tap in range(9):
        lhs = acts[tap % 3, pl.ds(TAP_OFF[tap // 3] * cols, 2 * cols)]
        part[tap * chans : (tap + 1) * chans] = dot(lhs, grad_rows, ((0,), (0,))).astype(bf16)

    half_rows = half.shape[1]
    core_cp = []
    for q in range(nz):
        core_cp.append(
            remote(
                part.at[pl.ds(aligned(q * block + 2 * step * (1 - ci)), half_rows)],
                core_in.at[q],
                core_sem.at[q],
                {"rep": core_peer},
            )
        )
        core_cp[q].start()

    fwd_x, fwd_c, fwd_d = [], [], []
    x_off = step * (2 * ci + 1 - xi)
    for d in range(nz - 1):
        w_cp[d].wait_recv()
        src_z = lax.rem(z + nz - 1 - d, nz)
        spot = wfull.at[pl.ds(aligned(src_z * block + my_off), step)]
        fwd_x.append(remote(spot, spot, w_sem.at[1, d], {"rep": x_peer}))
        fwd_c.append(remote(spot, spot, w_sem.at[2, d], {"rep": core_peer}))
        fwd_x[d].start()
        fwd_c[d].start()

    x_cp = []
    for q in range(nz):
        core_cp[q].wait_recv()
        mine_rows = part[pl.ds(aligned(q * block + 2 * step * ci), half_rows)]
        half[q] = (mine_rows.astype(f32) + core_in[q].astype(f32)).astype(bf16)
        x_cp.append(
            remote(
                half.at[q, pl.ds(aligned(step * (1 - xi)), quart)],
                x_in.at[q],
                x_sem.at[q],
                {"rep": x_peer},
            )
        )
        x_cp[q].start()

    for d in range(nz - 1):
        fwd_x[d].wait_recv()
        src_z = lax.rem(z + nz - 1 - d, nz)
        spot = wfull.at[pl.ds(aligned(src_z * block + x_off), step)]
        fwd_d.append(remote(spot, spot, w_sem.at[3, d], {"rep": core_peer}))
        fwd_d[d].start()
    own_w.wait()
    for d in range(nz - 1):
        tail_cp[d].wait_recv()
        fwd_c[d].wait_recv()
        fwd_d[d].wait_recv()

    result = jnp.zeros((2 * cols, wfull.shape[1]), f32)
    for tap in range(9):
        lhs = acts[tap % 3, pl.ds(TAP_OFF[tap // 3] * cols, 2 * cols)]
        result = result + dot(lhs, wfull[tap * chans : (tap + 1) * chans])
    out_ref[0, 0] = result[:cols].astype(bf16)
    out_ref[0, 1] = result[cols:].astype(bf16)

    u_sum = jnp.zeros((1, chans), f32)
    v_sum = jnp.zeros((1, chans), f32)

    def back(source, first, tap):
        lhs = source[first * cols : (first + 2) * cols]
        return dot(lhs, wfull[tap * chans : (tap + 1) * chans], ((1,), (1,)))

    for odd_row in range(2):
        for odd in range(2):
            if odd_row == 0 and odd == 0:
                grad = back(cts, 0, 4)
            elif odd_row == 0:
                grad = back(cts, 0, 5) + back(css, 0, 3)
            elif odd == 0:
                grad = back(cts, 0, 7) + back(cts, 1, 1)
            else:
                grad = back(cts, 0, 8) + back(css, 0, 6) + back(cts, 1, 2) + back(css, 1, 0)
            for i in range(2):
                r = 2 * i + odd_row
                part_rows = pl.ds(odd * cols, cols)
                value = grad[i * cols : (i + 1) * cols] * dsilu[r, part_rows]
                zgrad[r, part_rows] = value
                u_sum = u_sum + jnp.sum(value * norm[r + 1, part_rows], axis=0, keepdims=True)
                v_sum = v_sum + jnp.sum(value, axis=0, keepdims=True)
    uv[...] = jnp.zeros(uv.shape, f32)
    uv[0:1] = u_sum
    uv[1:2] = v_sum
    uv_cp = [remote(uv, uv_in.at[d], uv_sem.at[d], {"fsdp": peers_z[d]}) for d in range(nz - 1)]
    for cp in uv_cp:
        cp.start()

    for q in range(nz):
        x_cp[q].wait_recv()
        mine_rows = half[q, pl.ds(aligned(step * xi), quart)]
        quarter[q] = (mine_rows.astype(f32) + x_in[q].astype(f32)).astype(bf16)
    z_cp = []
    for d in range(nz - 1):
        z_cp.append(
            remote(quarter.at[peers_z[d]], z_in.at[d], z_sem.at[d], {"fsdp": peers_z[d]})
        )
        z_cp[d].start()

    for cp in uv_cp:
        cp.wait_recv()
    total = uv[...]
    for d in range(nz - 1):
        total = total + uv_in[d]
    uvt[...] = total
    uvt_cp = [remote(uvt, uvt_in.at[m], uvt_sem.at[m], {"rep": reps[m]}) for m in range(3)]
    for cp in uvt_cp:
        cp.start()
    grp = dot(gain * total, same, precision=lax.Precision.HIGHEST)
    su_val = grp[0:1] / count
    sv_val = grp[1:2] / count
    for r in range(rows):
        value = rstd * (gain * zgrad[r] - sv_val - norm[r + 1] * su_val)
        dx_ref[0, r] = dot(merge, value.astype(bf16)).astype(bf16)

    value = quarter[z].astype(f32)
    for d in range(nz - 1):
        z_cp[d].wait_recv()
        value = value + z_in[d].astype(f32)
    final[...] = (value * scale).astype(bf16)
    rep_cp = [remote(final, rep_in.at[m], rep_sem.at[m], {"rep": reps[m]}) for m in range(3)]
    for cp in rep_cp:
        cp.start()

    def place(ref, k):
        wg_ref[pl.ds(pl.multiple_of(step * k, 16), step)] = ref[0:step].astype(f32)

        @pl.when(k == 3)
        def _():
            wg_ref[4 * step : block] = ref[step:quart].astype(f32)

    place(final, mine)
    for cp in uvt_cp:
        cp.wait_recv()
    gg_ref[...] = (uvt[0:2] + uvt_in[0, 0:2] + uvt_in[1, 0:2] + uvt_in[2, 0:2]) * scale
    owners = [2 * (1 - ci) + xi, 2 * ci + 1 - xi, 2 * (1 - ci) + 1 - xi]
    for m in range(3):
        rep_cp[m].wait_recv()
        place(rep_in.at[m], owners[m])

    @pl.when(z < nz - 1)
    def _():
        halo_x.wait_send()

    @pl.when(z > 0)
    def _():
        halo_c.wait_send()

    for group in (
        stat_cp, w_cp, tail_cp, core_cp, fwd_x, fwd_c, fwd_d, x_cp, uv_cp, z_cp, uvt_cp, rep_cp
    ):
        for cp in group:
            cp.wait_send()


def fused_shards(images, gains, conv_weight, cotangent):
    batch, rows, width, chans = images.shape
    outs_ch = conv_weight.shape[1]
    nz = lax.axis_size("fsdp")
    block = conv_weight.shape[0]
    cols = width // 2
    tiles = block // 16
    step = 16 * (tiles // 4)
    quart = block - 3 * step
    f32, bf16 = jnp.float32, jnp.bfloat16
    vmem = pltpu.VMEM
    dma = pltpu.SemaphoreType.DMA
    return pl.pallas_call(
        functools.partial(fused, nz),
        out_shape=(
            jax.ShapeDtypeStruct((batch, rows // 2, cols, outs_ch), bf16),
            jax.ShapeDtypeStruct(images.shape, bf16),
            jax.ShapeDtypeStruct((block, outs_ch), f32),
            jax.ShapeDtypeStruct(gains.shape, f32),
        ),
        in_specs=[pl.BlockSpec(memory_space=vmem)] * 4,
        out_specs=[pl.BlockSpec(memory_space=vmem)] * 4,
        scratch_shapes=[
            vmem((width, chans), bf16),
            vmem((cols, outs_ch), bf16),
            vmem((rows + 1, width, chans), f32),
            vmem((rows, width, chans), f32),
            vmem((rows, width, chans), f32),
            vmem((3, 5 * cols, chans), bf16),
            vmem((3 * cols, outs_ch), bf16),
            vmem((3 * cols, outs_ch), bf16),
            vmem((nz * block, outs_ch), bf16),
            vmem((8, chans), f32),
            vmem((nz - 1, 8, chans), f32),
            vmem((nz * block, outs_ch), bf16),
            vmem((nz, step + quart, outs_ch), bf16),
            vmem((nz, step + quart, outs_ch), bf16),
            vmem((nz, quart, outs_ch), bf16),
            vmem((nz, quart, outs_ch), bf16),
            vmem((nz - 1, quart, outs_ch), bf16),
            vmem((quart, outs_ch), bf16),
            vmem((3, quart, outs_ch), bf16),
            vmem((8, chans), f32),
            vmem((nz - 1, 8, chans), f32),
            vmem((8, chans), f32),
            vmem((3, 8, chans), f32),
            dma((2, 2)),
            dma((nz - 1, 2)),
            dma((4, nz - 1, 2)),
            dma((nz - 1, 2)),
            dma((nz, 2)),
            dma((nz, 2)),
            dma((nz - 1, 2)),
            dma((3, 2)),
            dma((nz - 1, 2)),
            dma((3, 2)),
            dma((1,)),
        ],
        compiler_params=pltpu.CompilerParams(
            collective_id=0, has_side_effects=True, vmem_limit_bytes=48 * 1024 * 1024
        ),
    )(images, gains, conv_weight, cotangent)


def solution(mesh):
    in_specs = (
        P(("groups", "rep"), "fsdp", None, None),
        P(),
        P("fsdp", None),
        P(("groups", "rep"), "fsdp", None, None),
    )
    out_specs = (
        P(("groups", "rep"), "fsdp", None, None),
        P(("groups", "rep"), "fsdp", None, None),
        P(("groups", "fsdp"), None),
        P("groups", None),
    )
    small = mesh.shape["rep"] == 4 and mesh.shape["fsdp"] <= 4
    body = fused_shards if small else shards
    return jax.shard_map(body, mesh=mesh, in_specs=in_specs, out_specs=out_specs, check_vma=False)
```

```python
import functools

import jax
import jax.numpy as jnp
from jax import lax
from jax.experimental import pallas as pl
from jax.experimental.pallas import tpu as pltpu
from jax.sharding import PartitionSpec as P

GROUPS = 32
MESH = pl.DeviceIdType.MESH


def passed_along(shard, axis, by):
    size = lax.axis_size(axis)
    pairs = [(i, i + by) for i in range(size) if 0 <= i + by < size]
    return lax.ppermute(shard, axis, pairs)


def spread_taps(first, middle, last, axis):
    length = first.shape[axis]
    widths_end = [(0, 0)] * first.ndim
    widths_end[axis] = (0, 1)
    widths_start = [(0, 0)] * first.ndim
    widths_start[axis] = (1, 0)
    even = jnp.pad(first, widths_end) + jnp.pad(last, widths_start)
    odd = jnp.pad(middle, widths_end)
    merged = jnp.stack([even, odd], axis=axis + 1)
    shape = list(even.shape)
    shape[axis] = 2 * (length + 1)
    merged = merged.reshape(shape)
    return lax.slice_in_dim(merged, 0, 2 * length + 1, axis=axis)


def shards(images, gains, conv_weight, cotangent):
    batch, rows, width, chans = images.shape
    outs_ch = conv_weight.shape[1]
    n_fsdp = lax.axis_size("fsdp")
    per_group = chans // GROUPS
    x_val = images.astype(jnp.float32)
    grouped = x_val.reshape(batch, rows, width, GROUPS, per_group)
    part_one = jnp.sum(grouped, axis=(1, 2, 4))
    part_two = jnp.sum(grouped * grouped, axis=(1, 2, 4))
    full_weight = lax.all_gather(conv_weight, "fsdp", axis=0, tiled=True)
    sum_one, sum_two = lax.psum((part_one, part_two), "fsdp")
    count = rows * n_fsdp * width * per_group
    mean = sum_one / count
    rstd = 1.0 / jnp.sqrt(sum_two / count - mean * mean + 1e-05)
    normed_g = (grouped - mean[:, None, None, :, None]) * rstd[:, None, None, :, None]
    normed = normed_g.reshape(x_val.shape)
    z_val = gains[0] * normed + gains[1]
    act = (z_val * jax.nn.sigmoid(z_val)).astype(jnp.bfloat16)
    above = passed_along(act[:, rows - 1 : rows], "fsdp", 1)
    padded = jnp.concatenate([above, act], axis=1)
    kernel = full_weight.reshape(3, 3, chans, outs_ch)
    result = lax.conv_general_dilated(
        padded,
        kernel,
        (2, 2),
        ((0, 0), (1, 0)),
        dimension_numbers=("NHWC", "HWIO", "NHWC"),
        preferred_element_type=jnp.float32,
    )
    output_maps = result.astype(jnp.bfloat16)
    patch_grad = jnp.einsum(
        "bijo,ko->bijk", cotangent, full_weight, preferred_element_type=jnp.float32
    )
    half_rows, half_cols = (cotangent.shape[1], cotangent.shape[2])
    taps = patch_grad.reshape(batch, half_rows, half_cols, 3, 3, chans)
    by_row = [
        spread_taps(
            taps[:, :, :, row_tap, 0], taps[:, :, :, row_tap, 1], taps[:, :, :, row_tap, 2], 2
        )
        for row_tap in range(3)
    ]
    grid = spread_taps(by_row[0], by_row[1], by_row[2], 1)[:, :, 1:]
    from_below = passed_along(grid[:, 0:1].astype(jnp.bfloat16), "fsdp", -1).astype(jnp.float32)
    filler = jnp.zeros((batch, rows - 1, width, chans), jnp.float32)
    act_grad = grid[:, 1:] + jnp.concatenate([filler, from_below], axis=1)
    padded_cols = jnp.pad(padded, ((0, 0), (0, 0), (1, 0), (0, 0)))
    blocks = []
    for row_tap in range(3):
        for col_tap in range(3):
            window = padded_cols[:, row_tap : row_tap + rows : 2, col_tap : col_tap + width : 2]
            blocks.append(
                jnp.einsum("bijc,bijo->co", window, cotangent, preferred_element_type=jnp.float32)
            )
    total_pixels = batch * lax.axis_size("rep") * half_rows * n_fsdp * half_cols
    scale = 1.0 / jnp.sqrt(jnp.float32(total_pixels))
    weight_term = jnp.concatenate(blocks, axis=0) * scale
    sig = jax.nn.sigmoid(z_val)
    z_grad = act_grad * sig * (1.0 + z_val * (1.0 - sig))
    u_part = jnp.sum(z_grad * normed, axis=(1, 2))
    v_part = jnp.sum(z_grad, axis=(1, 2))
    u_sum, v_sum = lax.psum((u_part, v_part), "fsdp")
    gain_term = jnp.stack([jnp.sum(u_sum, axis=0), jnp.sum(v_sum, axis=0)]) * scale
    su_val = jnp.sum((gains[0] * u_sum).reshape(batch, GROUPS, per_group), axis=-1)
    sv_val = jnp.sum((gains[0] * v_sum).reshape(batch, GROUPS, per_group), axis=-1)
    scaled = (gains[0] * z_grad).reshape(grouped.shape)
    dx_val = rstd[:, None, None, :, None] * (
        scaled
        - sv_val[:, None, None, :, None] / count
        - normed_g * su_val[:, None, None, :, None] / count
    )
    input_grad = dx_val.reshape(x_val.shape).astype(jnp.bfloat16)
    owned = lax.psum_scatter(weight_term, "fsdp", scatter_dimension=0, tiled=True)
    weight_grad, gain_grad = (
        lax.psum(owned.astype(jnp.bfloat16), "rep").astype(jnp.float32),
        lax.psum(gain_term.astype(jnp.bfloat16), "rep").astype(jnp.float32),
    )
    return (output_maps, input_grad, weight_grad, gain_grad)


HIGHEST = lax.Precision.HIGHEST


def dot(lhs, rhs, contract=((1,), (0,)), precision=None):
    return lax.dot_general(
        lhs, rhs, (contract, ((), ())), precision=precision, preferred_element_type=jnp.float32
    )


def fused(
    nz,
    x_ref,
    g_ref,
    w_ref,
    ct_ref,
    out_ref,
    dx_ref,
    wg_ref,
    gg_ref,
    xh,
    cth,
    norm,
    dsilu,
    zgrad,
    patches,
    cts,
    taps,
    edge,
    wfull,
    stat,
    stat_in,
    part,
    core_in,
    half,
    x_in,
    quarter,
    z_in,
    final,
    rep_in,
    uv,
    uv_in,
    uvt,
    uvt_in,
    halo_sem,
    stat_sem,
    w_sem,
    core_sem,
    x_sem,
    z_sem,
    rep_sem,
    uv_sem,
    uvt_sem,
    loc_sem,
):
    f32, bf16 = jnp.float32, jnp.bfloat16
    rows, chans, width = x_ref.shape[1:]
    cols = width // 2
    outs_ch, block = w_ref.shape
    q_rows = outs_ch // 4
    h_rows = outs_ch // 2
    count = rows * nz * width * (chans // GROUPS)
    scale = 1.0 / jnp.sqrt(f32(4 * nz * ct_ref.shape[1] * cols))
    z = lax.axis_index("fsdp")
    rep = lax.axis_index("rep")
    yi = lax.axis_index("groups")
    xi, ci = rep // 2, rep % 2
    mine = 2 * ci + xi
    peers_z = [lax.rem(z + d, nz) for d in range(1, nz)]
    reps = [(2 * xi + 1 - ci), (2 * (1 - xi) + ci), (2 * (1 - xi) + 1 - ci)]
    core_peer, x_peer = reps[0], reps[1]
    order = [2, 1] + list(range(3, nz)) + [0]

    def aligned(value):
        return pl.multiple_of(value, 16)

    def remote(src, dst, sem, device):
        return pltpu.make_async_remote_copy(
            src_ref=src,
            dst_ref=dst,
            send_sem=sem.at[0],
            recv_sem=sem.at[1],
            device_id=device,
            device_id_type=MESH,
        )

    barrier = pltpu.get_barrier_semaphore()
    for peer in peers_z:
        pl.semaphore_signal(barrier, inc=1, device_id={"fsdp": peer}, device_id_type=MESH)
    for peer in reps:
        pl.semaphore_signal(barrier, inc=1, device_id={"rep": peer}, device_id_type=MESH)
    pl.semaphore_signal(barrier, inc=1, device_id={"groups": 1 - yi}, device_id_type=MESH)

    own_w = pltpu.make_async_copy(w_ref, wfull.at[z], loc_sem.at[0])
    own_w.start()

    big_i = lax.broadcasted_iota(jnp.int32, (width, width), 0)
    big_j = lax.broadcasted_iota(jnp.int32, (width, width), 1)
    split = jnp.where(
        jnp.where(big_j < cols, 2 * big_j, 2 * (big_j - cols) + 1) == big_i, 1.0, 0.0
    ).astype(bf16)
    merge = jnp.where(
        jnp.where(big_i < cols, 2 * big_i, 2 * (big_i - cols) + 1) == big_j, 1.0, 0.0
    ).astype(bf16)
    inv = 1.0 / (chans // GROUPS)
    ch_i = lax.broadcasted_iota(jnp.int32, (chans, chans), 0)
    ch_j = lax.broadcasted_iota(jnp.int32, (chans, chans), 1)
    grp_i = jnp.floor((ch_i.astype(f32) + 0.5) * inv)
    grp_j = jnp.floor((ch_j.astype(f32) + 0.5) * inv)
    same = jnp.where(grp_i == grp_j, 1.0, 0.0)
    eye = jnp.where(ch_i == ch_j, 1.0, 0.0)
    ones = jnp.ones((8, cols), f32)

    def row_sums(value):
        return dot(ones, value, ((1,), (1,)), HIGHEST)

    sum_one = jnp.zeros((chans, cols), f32)
    sum_two = jnp.zeros((chans, cols), f32)
    for r in range(rows):
        x_val = dot(x_ref[0, r], split)
        norm[r + 1] = x_val
        even, odd = x_val[:, :cols], x_val[:, cols:]
        sum_one = sum_one + (even + odd)
        sum_two = sum_two + (even * even + odd * odd)
    stat[0:8] = row_sums(sum_one)
    stat[8:16] = row_sums(sum_two)

    pl.semaphore_wait(barrier, nz - 1 + 3 + 1)

    stat_cp = [
        remote(stat, stat_in.at[d], stat_sem.at[d], {"fsdp": peers_z[d]}) for d in range(nz - 1)
    ]
    for cp in stat_cp:
        cp.start()

    halo_x = remote(x_ref.at[0, rows - 1], xh, halo_sem.at[0], {"fsdp": lax.rem(z + 1, nz)})
    halo_c = remote(ct_ref.at[0, 0], cth, halo_sem.at[1], {"fsdp": lax.rem(z + nz - 1, nz)})

    @pl.when(z < nz - 1)
    def _():
        halo_x.start()

    @pl.when(z > 0)
    def _():
        halo_c.start()

    w_off = aligned(q_rows * (2 * ci + yi))
    w_cp = []
    for d in range(nz - 1):
        w_cp.append(
            remote(
                w_ref.at[pl.ds(w_off, q_rows)],
                wfull.at[z, pl.ds(w_off, q_rows)],
                w_sem.at[0, d],
                {"fsdp": peers_z[d]},
            )
        )
        w_cp[d].start()

    lane = lax.broadcasted_iota(jnp.int32, (chans, cols), 1)

    @pl.when(z == nz - 1)
    def _():
        cth[...] = jnp.zeros(cth.shape, bf16)

    @pl.when(z == 0)
    def _():
        xh[...] = jnp.zeros(xh.shape, bf16)

    for i in range(2):
        cts[:, i * cols : (i + 1) * cols] = ct_ref[0, i]
    gains = dot(eye, g_ref[...], ((1,), (1,)), HIGHEST)
    gain = jnp.broadcast_to(gains[:, 0:1], (chans, cols))
    shift = jnp.broadcast_to(gains[:, 1:2], (chans, cols))

    for cp in stat_cp:
        cp.wait_recv()
    total = stat[...]
    for d in range(nz - 1):
        total = total + stat_in[d]
    total = dot(same, total, ((1,), (1,)), HIGHEST)
    mean = total[:, 0:1] / count
    rstd = 1.0 / jnp.sqrt(total[:, 8:9] / count - mean * mean + 1e-05)
    mean = jnp.broadcast_to(mean, (chans, cols))
    rstd = jnp.broadcast_to(rstd, (chans, cols))

    def put(row_tap, col_tap, i, value):
        tap = 3 * row_tap + col_tap
        patches[tap * chans : (tap + 1) * chans, i * cols : (i + 1) * cols] = value

    users = [[(t, i) for i in range(2) for t in range(3) if 2 * i + t == r] for r in range(5)]
    for r in (1, 2, 3, 4, 0):
        if r == 0:

            @pl.when(z > 0)
            def _():
                halo_x.wait_recv()

            norm[0] = dot(xh[...], split)
        for odd in range(2):
            here = pl.ds(odd * cols, cols)
            normed = (norm[r, :, here] - mean) * rstd
            z_val = gain * normed + shift
            sig = 0.5 * jnp.tanh(0.5 * z_val) + 0.5
            act = z_val * sig
            if r == 0:
                act = act * jnp.where(z > 0, 1.0, 0.0)
            else:
                norm[r, :, here] = normed
                dsilu[r - 1, :, here] = sig * (1.0 + z_val * (1.0 - sig))
            rounded = act.astype(bf16)
            for t, i in users[r]:
                put(t, 1 + odd, i, rounded)
            if odd == 1:
                moved = pltpu.roll(act, 1, axis=1)
                moved = jnp.where(lane == 0, 0.0, moved).astype(bf16)
                for t, i in users[r]:
                    put(t, 0, i, moved)

    fwd_y, fwd_c, fwd_d = [], [], []

    def forward_first(d):
        w_cp[d].wait_recv()
        src_z = lax.rem(z + nz - 1 - d, nz)
        spot = wfull.at[src_z, pl.ds(w_off, q_rows)]
        fwd_y.append(remote(spot, spot, w_sem.at[1, d], {"groups": 1 - yi}))
        fwd_c.append(remote(spot, spot, w_sem.at[2, d], {"rep": core_peer}))
        fwd_y[d].start()
        fwd_c[d].start()

    def forward_second(d):
        fwd_y[d].wait_recv()
        src_z = lax.rem(z + nz - 1 - d, nz)
        spot = wfull.at[src_z, pl.ds(aligned(q_rows * (2 * ci + 1 - yi)), q_rows)]
        fwd_d.append(remote(spot, spot, w_sem.at[3, d], {"rep": core_peer}))
        fwd_d[d].start()

    core_cp, x_cp, z_cp = [], [], []

    def core_step(n):
        d = order[n]
        q = lax.rem(z + d, nz)
        core_cp[n].wait_recv()
        mine_rows = part[q, pl.ds(aligned(h_rows * ci), h_rows)]
        half[n] = (mine_rows.astype(f32) + core_in[n].astype(f32)).astype(bf16)
        x_cp.append(
            remote(
                half.at[n, pl.ds(aligned(q_rows * (1 - xi)), q_rows)],
                x_in.at[n],
                x_sem.at[n],
                {"rep": x_peer},
            )
        )
        x_cp[n].start()

    def x_step(n):
        d = order[n]
        x_cp[n].wait_recv()
        mine_rows = half[n, pl.ds(aligned(q_rows * xi), q_rows)]
        value = mine_rows.astype(f32) + x_in[n].astype(f32)
        quarter[n] = value.astype(bf16)
        if d > 0:
            z_cp.append(
                remote(quarter.at[n], z_in.at[d - 1], z_sem.at[d - 1], {"fsdp": peers_z[d - 1]})
            )
            z_cp[n].start()

    for n, d in enumerate(order):
        q = lax.rem(z + d, nz)
        rhs = patches[pl.ds(aligned(q * block), block)]
        part[q] = dot(cts[:, : 2 * cols], rhs, ((1,), (1,))).astype(bf16)
        core_cp.append(
            remote(
                part.at[q, pl.ds(aligned(h_rows * (1 - ci)), h_rows)],
                core_in.at[n],
                core_sem.at[n],
                {"rep": core_peer},
            )
        )
        core_cp[n].start()
        if n > 0:
            core_step(n - 1)
    core_step(nz - 1)
    for d in range(nz - 1):
        forward_first(d)
    x_step(0)
    for d in range(nz - 1):
        forward_second(d)
    x_step(1)
    own_w.wait()
    for d in range(nz - 1):
        fwd_c[d].wait_recv()
        fwd_d[d].wait_recv()

    grads = cts[:, : 2 * cols]
    result = jnp.zeros((outs_ch, 2 * cols), f32)
    for q in range(nz):
        result = result + dot(wfull[q], patches[q * block : (q + 1) * block])
    out_ref[0, 0] = result[:, :cols].astype(bf16)
    out_ref[0, 1] = result[:, cols:].astype(bf16)
    for n in range(2, nz):
        x_step(n)

    for q in range(nz):
        taps[q * block : (q + 1) * block] = dot(wfull[q], grads, ((0,), (0,)))

    @pl.when(z < nz - 1)
    def _():
        halo_c.wait_recv()

    below = cth[...]
    done = 0
    q = 0
    while done < 3 * chans:
        take = min(block, 3 * chans - done)
        edge[done : done + take] = dot(wfull[q, :, :take], below, ((0,), (0,)))
        done += take
        q += 1

    def tap_at(row_tap, col_tap, i):
        tap = 3 * row_tap + col_tap
        here = slice(tap * chans, (tap + 1) * chans)
        if i == 2:
            return edge[here]
        return taps[here, i * cols : (i + 1) * cols]

    u_sum = jnp.zeros((chans, cols), f32)
    v_sum = jnp.zeros((chans, cols), f32)
    for r in range(rows):
        pairs = [(t, i) for i in range(3) for t in range(3) if 2 * i + t == r + 1]
        for odd in range(2):
            here = pl.ds(odd * cols, cols)
            grad = sum(tap_at(t, 1 + odd, i) for t, i in pairs)
            if odd == 1:
                left = sum(tap_at(t, 0, i) for t, i in pairs)
                moved = pltpu.roll(left, cols - 1, axis=1)
                grad = grad + jnp.where(lane == cols - 1, 0.0, moved)
            value = grad * dsilu[r, :, here]
            zgrad[r, :, here] = value
            u_sum = u_sum + value * norm[r + 1, :, here]
            v_sum = v_sum + value
    uv[0:8] = row_sums(u_sum)
    uv[8:16] = row_sums(v_sum)
    uv_cp = [remote(uv, uv_in.at[d], uv_sem.at[d], {"fsdp": peers_z[d]}) for d in range(nz - 1)]
    for cp in uv_cp:
        cp.start()

    value = quarter[nz - 1].astype(f32)
    for n in range(nz - 1):
        z_cp[n].wait_recv()
    for d in range(nz - 1):
        value = value + z_in[d].astype(f32)
    final[...] = (value * scale).astype(bf16)
    rep_cp = [remote(final, rep_in.at[m], rep_sem.at[m], {"rep": reps[m]}) for m in range(2)]
    for cp in rep_cp:
        cp.start()

    for cp in uv_cp:
        cp.wait_recv()
    total = uv[...]
    for d in range(nz - 1):
        total = total + uv_in[d]
    uvt[...] = total
    uvt_cp = [remote(uvt, uvt_in.at[m], uvt_sem.at[m], {"rep": reps[m]}) for m in range(3)]
    for cp in uvt_cp:
        cp.start()
    grp = dot(same, g_ref[0:1] * total, ((1,), (1,)), HIGHEST)
    su_val = jnp.broadcast_to(grp[:, 0:1] / count, (chans, cols))
    sv_val = jnp.broadcast_to(grp[:, 8:9] / count, (chans, cols))
    rep_cp[1].wait_recv()
    rep_cp.append(remote(rep_in.at[1], rep_in.at[2], rep_sem.at[2], {"rep": core_peer}))
    rep_cp[2].start()

    for r in range(rows):
        for odd in range(2):
            here = pl.ds(odd * cols, cols)
            value = rstd * (gain * zgrad[r, :, here] - sv_val - norm[r + 1, :, here] * su_val)
            patches[r * chans : (r + 1) * chans, here] = value.astype(bf16)
        dx_ref[0, r] = dot(patches[r * chans : (r + 1) * chans], merge).astype(bf16)

    def place(ref, k):
        wg_ref[pl.ds(aligned(q_rows * k), q_rows)] = ref[...].astype(f32)

    place(final, mine)
    for cp in uvt_cp:
        cp.wait_recv()
    total = uvt[...] + uvt_in[0] + uvt_in[1] + uvt_in[2]
    gg_ref[0:1] = total[0:1] * scale
    gg_ref[1:2] = total[8:9] * scale
    owners = [2 * (1 - ci) + xi, 2 * ci + 1 - xi, 2 * (1 - ci) + 1 - xi]
    for m in range(3):
        if m != 1:
            rep_cp[m].wait_recv()
        place(rep_in.at[m], owners[m])

    @pl.when(z < nz - 1)
    def _():
        halo_x.wait_send()

    @pl.when(z > 0)
    def _():
        halo_c.wait_send()

    for group in (
        stat_cp, w_cp, core_cp, fwd_y, fwd_c, fwd_d, x_cp, uv_cp, z_cp, uvt_cp, rep_cp
    ):
        for cp in group:
            cp.wait_send()


def fused_shards(images, gains, conv_weight, cotangent):
    batch, rows, width, chans = images.shape
    block, outs_ch = conv_weight.shape
    if (batch, rows, cotangent.shape[1]) != (1, 4, 2) or block % 16 or outs_ch % 64:
        return shards(images, gains, conv_weight, cotangent)
    nz = lax.axis_size("fsdp")
    cols = width // 2
    q_rows = outs_ch // 4
    f32, bf16 = jnp.float32, jnp.bfloat16
    vmem = pltpu.VMEM
    dma = pltpu.SemaphoreType.DMA
    output_maps, input_grad, weight_grad, gain_grad = pl.pallas_call(
        functools.partial(fused, nz),
        out_shape=(
            jax.ShapeDtypeStruct((batch, rows // 2, outs_ch, cols), bf16),
            jax.ShapeDtypeStruct((batch, rows, chans, width), bf16),
            jax.ShapeDtypeStruct((outs_ch, block), f32),
            jax.ShapeDtypeStruct(gains.shape, f32),
        ),
        in_specs=[pl.BlockSpec(memory_space=vmem)] * 4,
        out_specs=[pl.BlockSpec(memory_space=vmem)] * 4,
        scratch_shapes=[
            vmem((chans, width), bf16),
            vmem((outs_ch, cols), bf16),
            vmem((rows + 1, chans, width), f32),
            vmem((rows, chans, width), f32),
            vmem((rows, chans, width), f32),
            vmem((nz * block, width), bf16),
            vmem((outs_ch, width), bf16),
            vmem((nz * block, width), f32),
            vmem((3 * chans, cols), f32),
            vmem((nz, outs_ch, block), bf16),
            vmem((16, chans), f32),
            vmem((nz - 1, 16, chans), f32),
            vmem((nz, outs_ch, block), bf16),
            vmem((nz, 2 * q_rows, block), bf16),
            vmem((nz, 2 * q_rows, block), bf16),
            vmem((nz, q_rows, block), bf16),
            vmem((nz, q_rows, block), bf16),
            vmem((nz - 1, q_rows, block), bf16),
            vmem((q_rows, block), bf16),
            vmem((3, q_rows, block), bf16),
            vmem((16, chans), f32),
            vmem((nz - 1, 16, chans), f32),
            vmem((16, chans), f32),
            vmem((3, 16, chans), f32),
            dma((2, 2)),
            dma((nz - 1, 2)),
            dma((4, nz - 1, 2)),
            dma((nz, 2)),
            dma((nz, 2)),
            dma((nz - 1, 2)),
            dma((3, 2)),
            dma((nz - 1, 2)),
            dma((3, 2)),
            dma((1,)),
        ],
        compiler_params=pltpu.CompilerParams(
            collective_id=0, has_side_effects=True, vmem_limit_bytes=48 * 1024 * 1024
        ),
    )(
        jnp.swapaxes(images, 2, 3),
        gains,
        conv_weight.T,
        jnp.swapaxes(cotangent, 2, 3),
    )
    return (
        jnp.swapaxes(output_maps, 2, 3),
        jnp.swapaxes(input_grad, 2, 3),
        weight_grad.T,
        gain_grad,
    )


def solution(mesh):
    in_specs = (
        P(("groups", "rep"), "fsdp", None, None),
        P(),
        P("fsdp", None),
        P(("groups", "rep"), "fsdp", None, None),
    )
    out_specs = (
        P(("groups", "rep"), "fsdp", None, None),
        P(("groups", "rep"), "fsdp", None, None),
        P(("groups", "fsdp"), None),
        P("groups", None),
    )
    small = mesh.shape["groups"] == 2 and mesh.shape["rep"] == 4 and mesh.shape["fsdp"] == 4
    body = fused_shards if small else shards
    return jax.shard_map(body, mesh=mesh, in_specs=in_specs, out_specs=out_specs, check_vma=False)
```

```python
import functools

import jax
import jax.numpy as jnp
from jax import lax
from jax.experimental import pallas as pl
from jax.experimental.pallas import tpu as pltpu
from jax.sharding import PartitionSpec as P

GROUPS = 32
MESH = pl.DeviceIdType.MESH


def passed_along(shard, axis, by):
    size = lax.axis_size(axis)
    pairs = [(i, i + by) for i in range(size) if 0 <= i + by < size]
    return lax.ppermute(shard, axis, pairs)


def spread_taps(first, middle, last, axis):
    length = first.shape[axis]
    widths_end = [(0, 0)] * first.ndim
    widths_end[axis] = (0, 1)
    widths_start = [(0, 0)] * first.ndim
    widths_start[axis] = (1, 0)
    even = jnp.pad(first, widths_end) + jnp.pad(last, widths_start)
    odd = jnp.pad(middle, widths_end)
    merged = jnp.stack([even, odd], axis=axis + 1)
    shape = list(even.shape)
    shape[axis] = 2 * (length + 1)
    merged = merged.reshape(shape)
    return lax.slice_in_dim(merged, 0, 2 * length + 1, axis=axis)


def shards(images, gains, conv_weight, cotangent):
    batch, rows, width, chans = images.shape
    outs_ch = conv_weight.shape[1]
    n_fsdp = lax.axis_size("fsdp")
    per_group = chans // GROUPS
    x_val = images.astype(jnp.float32)
    grouped = x_val.reshape(batch, rows, width, GROUPS, per_group)
    part_one = jnp.sum(grouped, axis=(1, 2, 4))
    part_two = jnp.sum(grouped * grouped, axis=(1, 2, 4))
    full_weight = lax.all_gather(conv_weight, "fsdp", axis=0, tiled=True)
    sum_one, sum_two = lax.psum((part_one, part_two), "fsdp")
    count = rows * n_fsdp * width * per_group
    mean = sum_one / count
    rstd = 1.0 / jnp.sqrt(sum_two / count - mean * mean + 1e-05)
    normed_g = (grouped - mean[:, None, None, :, None]) * rstd[:, None, None, :, None]
    normed = normed_g.reshape(x_val.shape)
    z_val = gains[0] * normed + gains[1]
    act = (z_val * jax.nn.sigmoid(z_val)).astype(jnp.bfloat16)
    above = passed_along(act[:, rows - 1 : rows], "fsdp", 1)
    padded = jnp.concatenate([above, act], axis=1)
    kernel = full_weight.reshape(3, 3, chans, outs_ch)
    result = lax.conv_general_dilated(
        padded,
        kernel,
        (2, 2),
        ((0, 0), (1, 0)),
        dimension_numbers=("NHWC", "HWIO", "NHWC"),
        preferred_element_type=jnp.float32,
    )
    output_maps = result.astype(jnp.bfloat16)
    patch_grad = jnp.einsum(
        "bijo,ko->bijk", cotangent, full_weight, preferred_element_type=jnp.float32
    )
    half_rows, half_cols = (cotangent.shape[1], cotangent.shape[2])
    taps = patch_grad.reshape(batch, half_rows, half_cols, 3, 3, chans)
    by_row = [
        spread_taps(
            taps[:, :, :, row_tap, 0], taps[:, :, :, row_tap, 1], taps[:, :, :, row_tap, 2], 2
        )
        for row_tap in range(3)
    ]
    grid = spread_taps(by_row[0], by_row[1], by_row[2], 1)[:, :, 1:]
    from_below = passed_along(grid[:, 0:1].astype(jnp.bfloat16), "fsdp", -1).astype(jnp.float32)
    filler = jnp.zeros((batch, rows - 1, width, chans), jnp.float32)
    act_grad = grid[:, 1:] + jnp.concatenate([filler, from_below], axis=1)
    padded_cols = jnp.pad(padded, ((0, 0), (0, 0), (1, 0), (0, 0)))
    blocks = []
    for row_tap in range(3):
        for col_tap in range(3):
            window = padded_cols[:, row_tap : row_tap + rows : 2, col_tap : col_tap + width : 2]
            blocks.append(
                jnp.einsum("bijc,bijo->co", window, cotangent, preferred_element_type=jnp.float32)
            )
    total_pixels = batch * lax.axis_size("rep") * half_rows * n_fsdp * half_cols
    scale = 1.0 / jnp.sqrt(jnp.float32(total_pixels))
    weight_term = jnp.concatenate(blocks, axis=0) * scale
    sig = jax.nn.sigmoid(z_val)
    z_grad = act_grad * sig * (1.0 + z_val * (1.0 - sig))
    u_part = jnp.sum(z_grad * normed, axis=(1, 2))
    v_part = jnp.sum(z_grad, axis=(1, 2))
    u_sum, v_sum = lax.psum((u_part, v_part), "fsdp")
    gain_term = jnp.stack([jnp.sum(u_sum, axis=0), jnp.sum(v_sum, axis=0)]) * scale
    su_val = jnp.sum((gains[0] * u_sum).reshape(batch, GROUPS, per_group), axis=-1)
    sv_val = jnp.sum((gains[0] * v_sum).reshape(batch, GROUPS, per_group), axis=-1)
    scaled = (gains[0] * z_grad).reshape(grouped.shape)
    dx_val = rstd[:, None, None, :, None] * (
        scaled
        - sv_val[:, None, None, :, None] / count
        - normed_g * su_val[:, None, None, :, None] / count
    )
    input_grad = dx_val.reshape(x_val.shape).astype(jnp.bfloat16)
    owned = lax.psum_scatter(weight_term, "fsdp", scatter_dimension=0, tiled=True)
    weight_grad, gain_grad = (
        lax.psum(owned.astype(jnp.bfloat16), "rep").astype(jnp.float32),
        lax.psum(gain_term.astype(jnp.bfloat16), "rep").astype(jnp.float32),
    )
    return (output_maps, input_grad, weight_grad, gain_grad)


HIGHEST = lax.Precision.HIGHEST


def dot(lhs, rhs, contract=((1,), (0,)), precision=None):
    return lax.dot_general(
        lhs, rhs, (contract, ((), ())), precision=precision, preferred_element_type=jnp.float32
    )


def fused(
    nz,
    x_ref,
    g_ref,
    w_ref,
    ct_ref,
    out_ref,
    dx_ref,
    wg_ref,
    gg_ref,
    xh,
    cth,
    norm,
    dsilu,
    zgrad,
    patches,
    cts,
    taps,
    edge,
    wfull,
    stat,
    stat_in,
    part,
    core_in,
    half,
    x_in,
    quarter,
    z_in,
    final,
    rep_in,
    uv,
    uv_in,
    uvt,
    uvt_in,
    halo_sem,
    stat_sem,
    w_sem,
    core_sem,
    x_sem,
    z_sem,
    rep_sem,
    uv_sem,
    uvt_sem,
    loc_sem,
):
    f32, bf16 = jnp.float32, jnp.bfloat16
    rows, chans, width = x_ref.shape[1:]
    cols = width // 2
    outs_ch, block = w_ref.shape
    q_rows = outs_ch // 4
    h_rows = outs_ch // 2
    count = rows * nz * width * (chans // GROUPS)
    scale = 1.0 / jnp.sqrt(f32(4 * nz * ct_ref.shape[1] * cols))
    z = lax.axis_index("fsdp")
    rep = lax.axis_index("rep")
    yi = lax.axis_index("groups")
    xi, ci = rep // 2, rep % 2
    mine = 2 * ci + xi
    peers_z = [lax.rem(z + d, nz) for d in range(1, nz)]
    reps = [(2 * xi + 1 - ci), (2 * (1 - xi) + ci), (2 * (1 - xi) + 1 - ci)]
    core_peer, x_peer = reps[0], reps[1]
    order = [2, 1] + list(range(3, nz)) + [0]

    def aligned(value):
        return pl.multiple_of(value, 16)

    def remote(src, dst, sem, device):
        return pltpu.make_async_remote_copy(
            src_ref=src,
            dst_ref=dst,
            send_sem=sem.at[0],
            recv_sem=sem.at[1],
            device_id=device,
            device_id_type=MESH,
        )

    barrier = pltpu.get_barrier_semaphore()
    for peer in peers_z:
        pl.semaphore_signal(barrier, inc=1, device_id={"fsdp": peer}, device_id_type=MESH)
    for peer in reps:
        pl.semaphore_signal(barrier, inc=1, device_id={"rep": peer}, device_id_type=MESH)
    pl.semaphore_signal(barrier, inc=1, device_id={"groups": 1 - yi}, device_id_type=MESH)

    own_w = pltpu.make_async_copy(w_ref, wfull.at[z], loc_sem.at[0])
    own_w.start()

    big_i = lax.broadcasted_iota(jnp.int32, (width, width), 0)
    big_j = lax.broadcasted_iota(jnp.int32, (width, width), 1)
    split = jnp.where(
        jnp.where(big_j < cols, 2 * big_j, 2 * (big_j - cols) + 1) == big_i, 1.0, 0.0
    ).astype(bf16)
    merge = jnp.where(
        jnp.where(big_i < cols, 2 * big_i, 2 * (big_i - cols) + 1) == big_j, 1.0, 0.0
    ).astype(bf16)
    inv = 1.0 / (chans // GROUPS)
    ch_i = lax.broadcasted_iota(jnp.int32, (chans, chans), 0)
    ch_j = lax.broadcasted_iota(jnp.int32, (chans, chans), 1)
    grp_i = jnp.floor((ch_i.astype(f32) + 0.5) * inv)
    grp_j = jnp.floor((ch_j.astype(f32) + 0.5) * inv)
    same = jnp.where(grp_i == grp_j, 1.0, 0.0)
    eye = jnp.where(ch_i == ch_j, 1.0, 0.0)
    ones = jnp.ones((8, cols), f32)

    def row_sums(value):
        return dot(ones, value, ((1,), (1,)), HIGHEST)

    sum_one = jnp.zeros((chans, cols), f32)
    sum_two = jnp.zeros((chans, cols), f32)
    for r in range(rows):
        x_val = dot(x_ref[0, r], split)
        norm[r + 1] = x_val
        even, odd = x_val[:, :cols], x_val[:, cols:]
        sum_one = sum_one + (even + odd)
        sum_two = sum_two + (even * even + odd * odd)
    stat[0:8] = row_sums(sum_one)
    stat[8:16] = row_sums(sum_two)

    pl.semaphore_wait(barrier, nz - 1 + 3 + 1)

    stat_cp = [
        remote(stat, stat_in.at[d], stat_sem.at[d], {"fsdp": peers_z[d]}) for d in range(nz - 1)
    ]
    for cp in stat_cp:
        cp.start()

    halo_x = remote(x_ref.at[0, rows - 1], xh, halo_sem.at[0], {"fsdp": lax.rem(z + 1, nz)})
    halo_c = remote(ct_ref.at[0, 0], cth, halo_sem.at[1], {"fsdp": lax.rem(z + nz - 1, nz)})

    @pl.when(z < nz - 1)
    def _():
        halo_x.start()

    @pl.when(z > 0)
    def _():
        halo_c.start()

    w_off = aligned(q_rows * (2 * ci + yi))
    w_cp = []
    for d in range(nz - 1):
        w_cp.append(
            remote(
                w_ref.at[pl.ds(w_off, q_rows)],
                wfull.at[z, pl.ds(w_off, q_rows)],
                w_sem.at[0, d],
                {"fsdp": peers_z[d]},
            )
        )

    for d in reversed(range(nz - 1)):
        w_cp[d].start()

    lane = lax.broadcasted_iota(jnp.int32, (chans, cols), 1)

    @pl.when(z == nz - 1)
    def _():
        cth[...] = jnp.zeros(cth.shape, bf16)

    @pl.when(z == 0)
    def _():
        xh[...] = jnp.zeros(xh.shape, bf16)

    for i in range(2):
        cts[:, i * cols : (i + 1) * cols] = ct_ref[0, i]
    gains = dot(eye, g_ref[...], ((1,), (1,)), HIGHEST)
    gain = jnp.broadcast_to(gains[:, 0:1], (chans, cols))
    shift = jnp.broadcast_to(gains[:, 1:2], (chans, cols))

    for cp in stat_cp:
        cp.wait_recv()
    total = stat[...]
    for d in range(nz - 1):
        total = total + stat_in[d]
    total = dot(same, total, ((1,), (1,)), HIGHEST)
    mean = total[:, 0:1] / count
    rstd = 1.0 / jnp.sqrt(total[:, 8:9] / count - mean * mean + 1e-05)
    mean = jnp.broadcast_to(mean, (chans, cols))
    rstd = jnp.broadcast_to(rstd, (chans, cols))

    def put(row_tap, col_tap, i, value):
        tap = 3 * row_tap + col_tap
        patches[tap * chans : (tap + 1) * chans, i * cols : (i + 1) * cols] = value

    users = [[(t, i) for i in range(2) for t in range(3) if 2 * i + t == r] for r in range(5)]
    for r in (1, 2, 3, 4, 0):
        if r == 0:

            @pl.when(z > 0)
            def _():
                halo_x.wait_recv()

            norm[0] = dot(xh[...], split)
        for odd in range(2):
            here = pl.ds(odd * cols, cols)
            normed = (norm[r, :, here] - mean) * rstd
            z_val = gain * normed + shift
            sig = 0.5 * jnp.tanh(0.5 * z_val) + 0.5
            act = z_val * sig
            if r == 0:
                act = act * jnp.where(z > 0, 1.0, 0.0)
            else:
                norm[r, :, here] = normed
                dsilu[r - 1, :, here] = sig * (1.0 + z_val * (1.0 - sig))
            rounded = act.astype(bf16)
            for t, i in users[r]:
                put(t, 1 + odd, i, rounded)
            if odd == 1:
                moved = pltpu.roll(act, 1, axis=1)
                moved = jnp.where(lane == 0, 0.0, moved).astype(bf16)
                for t, i in users[r]:
                    put(t, 0, i, moved)

    fwd_y, fwd_c, fwd_d = [], [], []

    def forward_first(d):
        w_cp[d].wait_recv()
        src_z = lax.rem(z + nz - 1 - d, nz)
        spot = wfull.at[src_z, pl.ds(w_off, q_rows)]
        fwd_y.append(remote(spot, spot, w_sem.at[1, d], {"groups": 1 - yi}))
        fwd_c.append(remote(spot, spot, w_sem.at[2, d], {"rep": core_peer}))
        fwd_y[d].start()
        fwd_c[d].start()

    def forward_second(d):
        fwd_y[d].wait_recv()
        src_z = lax.rem(z + nz - 1 - d, nz)
        spot = wfull.at[src_z, pl.ds(aligned(q_rows * (2 * ci + 1 - yi)), q_rows)]
        fwd_d.append(remote(spot, spot, w_sem.at[3, d], {"rep": core_peer}))
        fwd_d[d].start()

    core_cp, x_cp, z_cp = [], [], []

    def core_step(n):
        d = order[n]
        q = lax.rem(z + d, nz)
        core_cp[n].wait_recv()
        mine_rows = part[q, pl.ds(aligned(h_rows * ci), h_rows)]
        half[n] = (mine_rows.astype(f32) + core_in[n].astype(f32)).astype(bf16)
        x_cp.append(
            remote(
                half.at[n, pl.ds(aligned(q_rows * (1 - xi)), q_rows)],
                x_in.at[n],
                x_sem.at[n],
                {"rep": x_peer},
            )
        )
        x_cp[n].start()

    def x_step(n):
        d = order[n]
        x_cp[n].wait_recv()
        mine_rows = half[n, pl.ds(aligned(q_rows * xi), q_rows)]
        value = mine_rows.astype(f32) + x_in[n].astype(f32)
        quarter[n] = value.astype(bf16)
        if d > 0:
            z_cp.append(
                remote(quarter.at[n], z_in.at[d - 1], z_sem.at[d - 1], {"fsdp": peers_z[d - 1]})
            )
            z_cp[n].start()

    for n, d in enumerate(order):
        q = lax.rem(z + d, nz)
        rhs = patches[pl.ds(aligned(q * block), block)]
        part[q] = dot(cts[:, : 2 * cols], rhs, ((1,), (1,))).astype(bf16)
        core_cp.append(
            remote(
                part.at[q, pl.ds(aligned(h_rows * (1 - ci)), h_rows)],
                core_in.at[n],
                core_sem.at[n],
                {"rep": core_peer},
            )
        )
        core_cp[n].start()
        if n > 0:
            core_step(n - 1)
    core_step(nz - 1)
    for d in range(nz - 1):
        forward_first(d)
    x_step(0)
    for d in range(nz - 1):
        forward_second(d)
    for n in range(1, nz):
        x_step(n)
    own_w.wait()
    for d in range(nz - 1):
        fwd_c[d].wait_recv()
        fwd_d[d].wait_recv()

    grads = cts[:, : 2 * cols]
    result = jnp.zeros((outs_ch, 2 * cols), f32)
    for q in range(nz):
        result = result + dot(wfull[q], patches[q * block : (q + 1) * block])
    out_ref[0, 0] = result[:, :cols].astype(bf16)
    out_ref[0, 1] = result[:, cols:].astype(bf16)
    for q in range(nz):
        taps[q * block : (q + 1) * block] = dot(wfull[q], grads, ((0,), (0,)))

    @pl.when(z < nz - 1)
    def _():
        halo_c.wait_recv()

    below = cth[...]
    done = 0
    q = 0
    while done < 3 * chans:
        take = min(block, 3 * chans - done)
        edge[done : done + take] = dot(wfull[q, :, :take], below, ((0,), (0,)))
        done += take
        q += 1

    def tap_at(row_tap, col_tap, i):
        tap = 3 * row_tap + col_tap
        here = slice(tap * chans, (tap + 1) * chans)
        if i == 2:
            return edge[here]
        return taps[here, i * cols : (i + 1) * cols]

    u_sum = jnp.zeros((chans, cols), f32)
    v_sum = jnp.zeros((chans, cols), f32)
    for r in range(rows):
        pairs = [(t, i) for i in range(3) for t in range(3) if 2 * i + t == r + 1]
        for odd in range(2):
            here = pl.ds(odd * cols, cols)
            grad = sum(tap_at(t, 1 + odd, i) for t, i in pairs)
            if odd == 1:
                left = sum(tap_at(t, 0, i) for t, i in pairs)
                moved = pltpu.roll(left, cols - 1, axis=1)
                grad = grad + jnp.where(lane == cols - 1, 0.0, moved)
            value = grad * dsilu[r, :, here]
            zgrad[r, :, here] = value
            u_sum = u_sum + value * norm[r + 1, :, here]
            v_sum = v_sum + value
    uv[0:8] = row_sums(u_sum)
    uv[8:16] = row_sums(v_sum)
    uv_cp = [remote(uv, uv_in.at[d], uv_sem.at[d], {"fsdp": peers_z[d]}) for d in range(nz - 1)]
    for cp in uv_cp:
        cp.start()

    value = quarter[nz - 1].astype(f32)
    for n in range(nz - 1):
        z_cp[n].wait_recv()
    for d in range(nz - 1):
        value = value + z_in[d].astype(f32)
    final[...] = (value * scale).astype(bf16)
    rep_cp = [remote(final, rep_in.at[m], rep_sem.at[m], {"rep": reps[m]}) for m in range(2)]
    for cp in rep_cp:
        cp.start()

    for cp in uv_cp:
        cp.wait_recv()
    total = uv[...]
    for d in range(nz - 1):
        total = total + uv_in[d]
    uvt[...] = total
    uvt_cp = [remote(uvt, uvt_in.at[m], uvt_sem.at[m], {"rep": reps[m]}) for m in range(3)]
    for cp in uvt_cp:
        cp.start()
    grp = dot(same, g_ref[0:1] * total, ((1,), (1,)), HIGHEST)
    su_val = jnp.broadcast_to(grp[:, 0:1] / count, (chans, cols))
    sv_val = jnp.broadcast_to(grp[:, 8:9] / count, (chans, cols))
    rep_cp[1].wait_recv()
    rep_cp.append(remote(rep_in.at[1], rep_in.at[2], rep_sem.at[2], {"rep": core_peer}))
    rep_cp[2].start()

    for r in range(rows):
        for odd in range(2):
            here = pl.ds(odd * cols, cols)
            value = rstd * (gain * zgrad[r, :, here] - sv_val - norm[r + 1, :, here] * su_val)
            patches[r * chans : (r + 1) * chans, here] = value.astype(bf16)
        dx_ref[0, r] = dot(patches[r * chans : (r + 1) * chans], merge).astype(bf16)

    def place(ref, k):
        wg_ref[pl.ds(aligned(q_rows * k), q_rows)] = ref[...].astype(f32)

    place(final, mine)
    for cp in uvt_cp:
        cp.wait_recv()
    total = uvt[...] + uvt_in[0] + uvt_in[1] + uvt_in[2]
    gg_ref[0:1] = total[0:1] * scale
    gg_ref[1:2] = total[8:9] * scale
    owners = [2 * (1 - ci) + xi, 2 * ci + 1 - xi, 2 * (1 - ci) + 1 - xi]
    for m in range(3):
        if m != 1:
            rep_cp[m].wait_recv()
        place(rep_in.at[m], owners[m])

    @pl.when(z < nz - 1)
    def _():
        halo_x.wait_send()

    @pl.when(z > 0)
    def _():
        halo_c.wait_send()

    for group in (
        stat_cp, w_cp, core_cp, fwd_y, fwd_c, fwd_d, x_cp, uv_cp, z_cp, uvt_cp, rep_cp
    ):
        for cp in group:
            cp.wait_send()


def fused_shards(images, gains, conv_weight, cotangent):
    batch, rows, width, chans = images.shape
    block, outs_ch = conv_weight.shape
    if (batch, rows, cotangent.shape[1]) != (1, 4, 2) or block % 16 or outs_ch % 64:
        return shards(images, gains, conv_weight, cotangent)
    nz = lax.axis_size("fsdp")
    cols = width // 2
    q_rows = outs_ch // 4
    f32, bf16 = jnp.float32, jnp.bfloat16
    vmem = pltpu.VMEM
    dma = pltpu.SemaphoreType.DMA
    output_maps, input_grad, weight_grad, gain_grad = pl.pallas_call(
        functools.partial(fused, nz),
        out_shape=(
            jax.ShapeDtypeStruct((batch, rows // 2, outs_ch, cols), bf16),
            jax.ShapeDtypeStruct((batch, rows, chans, width), bf16),
            jax.ShapeDtypeStruct((outs_ch, block), f32),
            jax.ShapeDtypeStruct(gains.shape, f32),
        ),
        in_specs=[pl.BlockSpec(memory_space=vmem)] * 4,
        out_specs=[pl.BlockSpec(memory_space=vmem)] * 4,
        scratch_shapes=[
            vmem((chans, width), bf16),
            vmem((outs_ch, cols), bf16),
            vmem((rows + 1, chans, width), f32),
            vmem((rows, chans, width), f32),
            vmem((rows, chans, width), f32),
            vmem((nz * block, width), bf16),
            vmem((outs_ch, width), bf16),
            vmem((nz * block, width), f32),
            vmem((3 * chans, cols), f32),
            vmem((nz, outs_ch, block), bf16),
            vmem((16, chans), f32),
            vmem((nz - 1, 16, chans), f32),
            vmem((nz, outs_ch, block), bf16),
            vmem((nz, 2 * q_rows, block), bf16),
            vmem((nz, 2 * q_rows, block), bf16),
            vmem((nz, q_rows, block), bf16),
            vmem((nz, q_rows, block), bf16),
            vmem((nz - 1, q_rows, block), bf16),
            vmem((q_rows, block), bf16),
            vmem((3, q_rows, block), bf16),
            vmem((16, chans), f32),
            vmem((nz - 1, 16, chans), f32),
            vmem((16, chans), f32),
            vmem((3, 16, chans), f32),
            dma((2, 2)),
            dma((nz - 1, 2)),
            dma((4, nz - 1, 2)),
            dma((nz, 2)),
            dma((nz, 2)),
            dma((nz - 1, 2)),
            dma((3, 2)),
            dma((nz - 1, 2)),
            dma((3, 2)),
            dma((1,)),
        ],
        compiler_params=pltpu.CompilerParams(
            collective_id=0, has_side_effects=True, vmem_limit_bytes=48 * 1024 * 1024
        ),
    )(
        jnp.swapaxes(images, 2, 3),
        gains,
        conv_weight.T,
        jnp.swapaxes(cotangent, 2, 3),
    )
    return (
        jnp.swapaxes(output_maps, 2, 3),
        jnp.swapaxes(input_grad, 2, 3),
        weight_grad.T,
        gain_grad,
    )


def solution(mesh):
    in_specs = (
        P(("groups", "rep"), "fsdp", None, None),
        P(),
        P("fsdp", None),
        P(("groups", "rep"), "fsdp", None, None),
    )
    out_specs = (
        P(("groups", "rep"), "fsdp", None, None),
        P(("groups", "rep"), "fsdp", None, None),
        P(("groups", "fsdp"), None),
        P("groups", None),
    )
    small = mesh.shape["groups"] == 2 and mesh.shape["rep"] == 4 and mesh.shape["fsdp"] == 4
    body = fused_shards if small else shards
    return jax.shard_map(body, mesh=mesh, in_specs=in_specs, out_specs=out_specs, check_vma=False)
```

```python
import functools

import jax
import jax.numpy as jnp
from jax import lax
from jax.experimental import pallas as pl
from jax.experimental.pallas import tpu as pltpu
from jax.sharding import PartitionSpec as P

GROUPS = 32
MESH = pl.DeviceIdType.MESH


def passed_along(shard, axis, by):
    size = lax.axis_size(axis)
    pairs = [(i, i + by) for i in range(size) if 0 <= i + by < size]
    return lax.ppermute(shard, axis, pairs)


def spread_taps(first, middle, last, axis):
    length = first.shape[axis]
    widths_end = [(0, 0)] * first.ndim
    widths_end[axis] = (0, 1)
    widths_start = [(0, 0)] * first.ndim
    widths_start[axis] = (1, 0)
    even = jnp.pad(first, widths_end) + jnp.pad(last, widths_start)
    odd = jnp.pad(middle, widths_end)
    merged = jnp.stack([even, odd], axis=axis + 1)
    shape = list(even.shape)
    shape[axis] = 2 * (length + 1)
    merged = merged.reshape(shape)
    return lax.slice_in_dim(merged, 0, 2 * length + 1, axis=axis)


def shards(images, gains, conv_weight, cotangent):
    batch, rows, width, chans = images.shape
    outs_ch = conv_weight.shape[1]
    n_fsdp = lax.axis_size("fsdp")
    per_group = chans // GROUPS
    x_val = images.astype(jnp.float32)
    grouped = x_val.reshape(batch, rows, width, GROUPS, per_group)
    part_one = jnp.sum(grouped, axis=(1, 2, 4))
    part_two = jnp.sum(grouped * grouped, axis=(1, 2, 4))
    full_weight = lax.all_gather(conv_weight, "fsdp", axis=0, tiled=True)
    sum_one, sum_two = lax.psum((part_one, part_two), "fsdp")
    count = rows * n_fsdp * width * per_group
    mean = sum_one / count
    rstd = 1.0 / jnp.sqrt(sum_two / count - mean * mean + 1e-05)
    normed_g = (grouped - mean[:, None, None, :, None]) * rstd[:, None, None, :, None]
    normed = normed_g.reshape(x_val.shape)
    z_val = gains[0] * normed + gains[1]
    act = (z_val * jax.nn.sigmoid(z_val)).astype(jnp.bfloat16)
    above = passed_along(act[:, rows - 1 : rows], "fsdp", 1)
    padded = jnp.concatenate([above, act], axis=1)
    kernel = full_weight.reshape(3, 3, chans, outs_ch)
    result = lax.conv_general_dilated(
        padded,
        kernel,
        (2, 2),
        ((0, 0), (1, 0)),
        dimension_numbers=("NHWC", "HWIO", "NHWC"),
        preferred_element_type=jnp.float32,
    )
    output_maps = result.astype(jnp.bfloat16)
    patch_grad = jnp.einsum(
        "bijo,ko->bijk", cotangent, full_weight, preferred_element_type=jnp.float32
    )
    half_rows, half_cols = (cotangent.shape[1], cotangent.shape[2])
    taps = patch_grad.reshape(batch, half_rows, half_cols, 3, 3, chans)
    by_row = [
        spread_taps(
            taps[:, :, :, row_tap, 0], taps[:, :, :, row_tap, 1], taps[:, :, :, row_tap, 2], 2
        )
        for row_tap in range(3)
    ]
    grid = spread_taps(by_row[0], by_row[1], by_row[2], 1)[:, :, 1:]
    from_below = passed_along(grid[:, 0:1].astype(jnp.bfloat16), "fsdp", -1).astype(jnp.float32)
    filler = jnp.zeros((batch, rows - 1, width, chans), jnp.float32)
    act_grad = grid[:, 1:] + jnp.concatenate([filler, from_below], axis=1)
    padded_cols = jnp.pad(padded, ((0, 0), (0, 0), (1, 0), (0, 0)))
    blocks = []
    for row_tap in range(3):
        for col_tap in range(3):
            window = padded_cols[:, row_tap : row_tap + rows : 2, col_tap : col_tap + width : 2]
            blocks.append(
                jnp.einsum("bijc,bijo->co", window, cotangent, preferred_element_type=jnp.float32)
            )
    total_pixels = batch * lax.axis_size("rep") * half_rows * n_fsdp * half_cols
    scale = 1.0 / jnp.sqrt(jnp.float32(total_pixels))
    weight_term = jnp.concatenate(blocks, axis=0) * scale
    sig = jax.nn.sigmoid(z_val)
    z_grad = act_grad * sig * (1.0 + z_val * (1.0 - sig))
    u_part = jnp.sum(z_grad * normed, axis=(1, 2))
    v_part = jnp.sum(z_grad, axis=(1, 2))
    u_sum, v_sum = lax.psum((u_part, v_part), "fsdp")
    gain_term = jnp.stack([jnp.sum(u_sum, axis=0), jnp.sum(v_sum, axis=0)]) * scale
    su_val = jnp.sum((gains[0] * u_sum).reshape(batch, GROUPS, per_group), axis=-1)
    sv_val = jnp.sum((gains[0] * v_sum).reshape(batch, GROUPS, per_group), axis=-1)
    scaled = (gains[0] * z_grad).reshape(grouped.shape)
    dx_val = rstd[:, None, None, :, None] * (
        scaled
        - sv_val[:, None, None, :, None] / count
        - normed_g * su_val[:, None, None, :, None] / count
    )
    input_grad = dx_val.reshape(x_val.shape).astype(jnp.bfloat16)
    owned = lax.psum_scatter(weight_term, "fsdp", scatter_dimension=0, tiled=True)
    weight_grad, gain_grad = (
        lax.psum(owned.astype(jnp.bfloat16), "rep").astype(jnp.float32),
        lax.psum(gain_term.astype(jnp.bfloat16), "rep").astype(jnp.float32),
    )
    return (output_maps, input_grad, weight_grad, gain_grad)


HIGHEST = lax.Precision.HIGHEST


def dot(lhs, rhs, contract=((1,), (0,)), precision=None):
    return lax.dot_general(
        lhs, rhs, (contract, ((), ())), precision=precision, preferred_element_type=jnp.float32
    )


def fused(
    nz,
    x_ref,
    g_ref,
    w_ref,
    ct_ref,
    out_ref,
    dx_ref,
    wg_ref,
    gg_ref,
    xh,
    cth,
    norm,
    dsilu,
    zgrad,
    patches,
    cts,
    taps,
    edge,
    wfull,
    stat,
    stat_in,
    part,
    core_in,
    half,
    x_in,
    quarter,
    z_in,
    final,
    rep_in,
    uv,
    uv_in,
    uvt,
    uvt_in,
    halo_sem,
    stat_sem,
    w_sem,
    core_sem,
    x_sem,
    z_sem,
    rep_sem,
    uv_sem,
    uvt_sem,
    loc_sem,
):
    f32, bf16 = jnp.float32, jnp.bfloat16
    rows, chans, width = x_ref.shape[1:]
    cols = width // 2
    outs_ch, block = w_ref.shape
    q_rows = outs_ch // 4
    h_rows = outs_ch // 2
    count = rows * nz * width * (chans // GROUPS)
    scale = 1.0 / jnp.sqrt(f32(4 * nz * ct_ref.shape[1] * cols))
    z = lax.axis_index("fsdp")
    rep = lax.axis_index("rep")
    yi = lax.axis_index("groups")
    xi, ci = rep // 2, rep % 2
    mine = 2 * ci + xi
    peers_z = [lax.rem(z + d, nz) for d in range(1, nz)]
    reps = [(2 * xi + 1 - ci), (2 * (1 - xi) + ci), (2 * (1 - xi) + 1 - ci)]
    core_peer, x_peer = reps[0], reps[1]
    order = [2, 1] + list(range(3, nz)) + [0]

    def aligned(value):
        return pl.multiple_of(value, 16)

    def remote(src, dst, sem, device):
        return pltpu.make_async_remote_copy(
            src_ref=src,
            dst_ref=dst,
            send_sem=sem.at[0],
            recv_sem=sem.at[1],
            device_id=device,
            device_id_type=MESH,
        )

    barrier = pltpu.get_barrier_semaphore()
    for peer in peers_z:
        pl.semaphore_signal(barrier, inc=1, device_id={"fsdp": peer}, device_id_type=MESH)
    for peer in reps:
        pl.semaphore_signal(barrier, inc=1, device_id={"rep": peer}, device_id_type=MESH)
    pl.semaphore_signal(barrier, inc=1, device_id={"groups": 1 - yi}, device_id_type=MESH)

    own_w = pltpu.make_async_copy(w_ref, wfull.at[z], loc_sem.at[0])
    own_w.start()

    big_i = lax.broadcasted_iota(jnp.int32, (width, width), 0)
    big_j = lax.broadcasted_iota(jnp.int32, (width, width), 1)
    split = jnp.where(
        jnp.where(big_j < cols, 2 * big_j, 2 * (big_j - cols) + 1) == big_i, 1.0, 0.0
    ).astype(bf16)
    merge = jnp.where(
        jnp.where(big_i < cols, 2 * big_i, 2 * (big_i - cols) + 1) == big_j, 1.0, 0.0
    ).astype(bf16)
    inv = 1.0 / (chans // GROUPS)
    ch_i = lax.broadcasted_iota(jnp.int32, (chans, chans), 0)
    ch_j = lax.broadcasted_iota(jnp.int32, (chans, chans), 1)
    grp_i = jnp.floor((ch_i.astype(f32) + 0.5) * inv)
    grp_j = jnp.floor((ch_j.astype(f32) + 0.5) * inv)
    same = jnp.where(grp_i == grp_j, 1.0, 0.0)
    eye = jnp.where(ch_i == ch_j, 1.0, 0.0)
    ones = jnp.ones((8, cols), f32)

    def row_sums(value):
        return dot(ones, value, ((1,), (1,)), HIGHEST)

    sum_one = jnp.zeros((chans, cols), f32)
    sum_two = jnp.zeros((chans, cols), f32)
    for r in range(rows):
        x_val = dot(x_ref[0, r], split)
        norm[r + 1] = x_val
        even, odd = x_val[:, :cols], x_val[:, cols:]
        sum_one = sum_one + (even + odd)
        sum_two = sum_two + (even * even + odd * odd)
    stat[0:8] = row_sums(sum_one)
    stat[8:16] = row_sums(sum_two)

    pl.semaphore_wait(barrier, nz - 1 + 3 + 1)

    stat_cp = [
        remote(stat, stat_in.at[d], stat_sem.at[d], {"fsdp": peers_z[d]}) for d in range(nz - 1)
    ]
    for cp in stat_cp:
        cp.start()

    halo_x = remote(x_ref.at[0, rows - 1], xh, halo_sem.at[0], {"fsdp": lax.rem(z + 1, nz)})
    halo_c = remote(ct_ref.at[0, 0], cth, halo_sem.at[1], {"fsdp": lax.rem(z + nz - 1, nz)})

    @pl.when(z < nz - 1)
    def _():
        halo_x.start()

    w_off = aligned(q_rows * (2 * ci + yi))
    w_cp = []
    for d in range(nz - 1):
        w_cp.append(
            remote(
                w_ref.at[pl.ds(w_off, q_rows)],
                wfull.at[z, pl.ds(w_off, q_rows)],
                w_sem.at[0, d],
                {"fsdp": peers_z[d]},
            )
        )

    for d in reversed(range(nz - 1)):
        w_cp[d].start()

    @pl.when(z > 0)
    def _():
        halo_c.start()

    lane = lax.broadcasted_iota(jnp.int32, (chans, cols), 1)

    @pl.when(z == nz - 1)
    def _():
        cth[...] = jnp.zeros(cth.shape, bf16)

    @pl.when(z == 0)
    def _():
        xh[...] = jnp.zeros(xh.shape, bf16)

    for i in range(2):
        cts[:, i * cols : (i + 1) * cols] = ct_ref[0, i]
    gains = dot(eye, g_ref[...], ((1,), (1,)), HIGHEST)
    gain = jnp.broadcast_to(gains[:, 0:1], (chans, cols))
    shift = jnp.broadcast_to(gains[:, 1:2], (chans, cols))

    for cp in stat_cp:
        cp.wait_recv()
    total = stat[...]
    for d in range(nz - 1):
        total = total + stat_in[d]
    total = dot(same, total, ((1,), (1,)), HIGHEST)
    mean = total[:, 0:1] / count
    rstd = 1.0 / jnp.sqrt(total[:, 8:9] / count - mean * mean + 1e-05)
    mean = jnp.broadcast_to(mean, (chans, cols))
    rstd = jnp.broadcast_to(rstd, (chans, cols))

    def put(row_tap, col_tap, i, value):
        tap = 3 * row_tap + col_tap
        patches[tap * chans : (tap + 1) * chans, i * cols : (i + 1) * cols] = value

    users = [[(t, i) for i in range(2) for t in range(3) if 2 * i + t == r] for r in range(5)]
    for r in (1, 2, 3, 4, 0):
        if r == 0:

            @pl.when(z > 0)
            def _():
                halo_x.wait_recv()

            norm[0] = dot(xh[...], split)
        for odd in range(2):
            here = pl.ds(odd * cols, cols)
            normed = (norm[r, :, here] - mean) * rstd
            z_val = gain * normed + shift
            sig = 0.5 * jnp.tanh(0.5 * z_val) + 0.5
            act = z_val * sig
            if r == 0:
                act = act * jnp.where(z > 0, 1.0, 0.0)
            else:
                norm[r, :, here] = normed
                dsilu[r - 1, :, here] = sig * (1.0 + z_val * (1.0 - sig))
            rounded = act.astype(bf16)
            for t, i in users[r]:
                put(t, 1 + odd, i, rounded)
            if odd == 1:
                moved = pltpu.roll(act, 1, axis=1)
                moved = jnp.where(lane == 0, 0.0, moved).astype(bf16)
                for t, i in users[r]:
                    put(t, 0, i, moved)

    fwd_y, fwd_c, fwd_d = [], [], []

    def forward_first(d):
        w_cp[d].wait_recv()
        src_z = lax.rem(z + nz - 1 - d, nz)
        spot = wfull.at[src_z, pl.ds(w_off, q_rows)]
        fwd_y.append(remote(spot, spot, w_sem.at[1, d], {"groups": 1 - yi}))
        fwd_c.append(remote(spot, spot, w_sem.at[2, d], {"rep": core_peer}))
        fwd_y[d].start()
        fwd_c[d].start()

    def forward_second(d):
        fwd_y[d].wait_recv()
        src_z = lax.rem(z + nz - 1 - d, nz)
        spot = wfull.at[src_z, pl.ds(aligned(q_rows * (2 * ci + 1 - yi)), q_rows)]
        fwd_d.append(remote(spot, spot, w_sem.at[3, d], {"rep": core_peer}))
        fwd_d[d].start()

    core_cp, x_cp, z_cp = [], [], []

    def core_step(n):
        d = order[n]
        q = lax.rem(z + d, nz)
        core_cp[n].wait_recv()
        mine_rows = part[q, pl.ds(aligned(h_rows * ci), h_rows)]
        half[n] = (mine_rows.astype(f32) + core_in[n].astype(f32)).astype(bf16)
        x_cp.append(
            remote(
                half.at[n, pl.ds(aligned(q_rows * (1 - xi)), q_rows)],
                x_in.at[n],
                x_sem.at[n],
                {"rep": x_peer},
            )
        )
        x_cp[n].start()

    def x_step(n):
        d = order[n]
        x_cp[n].wait_recv()
        mine_rows = half[n, pl.ds(aligned(q_rows * xi), q_rows)]
        value = mine_rows.astype(f32) + x_in[n].astype(f32)
        quarter[n] = value.astype(bf16)
        if d > 0:
            z_cp.append(
                remote(quarter.at[n], z_in.at[d - 1], z_sem.at[d - 1], {"fsdp": peers_z[d - 1]})
            )
            z_cp[n].start()

    for n, d in enumerate(order):
        q = lax.rem(z + d, nz)
        rhs = patches[pl.ds(aligned(q * block), block)]
        part[q] = dot(cts[:, : 2 * cols], rhs, ((1,), (1,))).astype(bf16)
        core_cp.append(
            remote(
                part.at[q, pl.ds(aligned(h_rows * (1 - ci)), h_rows)],
                core_in.at[n],
                core_sem.at[n],
                {"rep": core_peer},
            )
        )
        core_cp[n].start()
        if n > 0:
            core_step(n - 1)
    core_step(nz - 1)
    for d in range(nz - 1):
        forward_first(d)
    x_step(0)
    for d in range(nz - 1):
        forward_second(d)
    for n in range(1, nz):
        x_step(n)
    own_w.wait()
    for d in range(nz - 1):
        fwd_c[d].wait_recv()
        fwd_d[d].wait_recv()

    grads = cts[:, : 2 * cols]
    result = jnp.zeros((outs_ch, 2 * cols), f32)
    for q in range(nz):
        result = result + dot(wfull[q], patches[q * block : (q + 1) * block])
    out_ref[0, 0] = result[:, :cols].astype(bf16)
    out_ref[0, 1] = result[:, cols:].astype(bf16)
    for q in range(nz):
        taps[q * block : (q + 1) * block] = dot(wfull[q], grads, ((0,), (0,)))

    @pl.when(z < nz - 1)
    def _():
        halo_c.wait_recv()

    below = cth[...]
    done = 0
    q = 0
    while done < 3 * chans:
        take = min(block, 3 * chans - done)
        edge[done : done + take] = dot(wfull[q, :, :take], below, ((0,), (0,)))
        done += take
        q += 1

    def tap_at(row_tap, col_tap, i):
        tap = 3 * row_tap + col_tap
        here = slice(tap * chans, (tap + 1) * chans)
        if i == 2:
            return edge[here]
        return taps[here, i * cols : (i + 1) * cols]

    u_sum = jnp.zeros((chans, cols), f32)
    v_sum = jnp.zeros((chans, cols), f32)
    for r in range(rows):
        pairs = [(t, i) for i in range(3) for t in range(3) if 2 * i + t == r + 1]
        for odd in range(2):
            here = pl.ds(odd * cols, cols)
            grad = sum(tap_at(t, 1 + odd, i) for t, i in pairs)
            if odd == 1:
                left = sum(tap_at(t, 0, i) for t, i in pairs)
                moved = pltpu.roll(left, cols - 1, axis=1)
                grad = grad + jnp.where(lane == cols - 1, 0.0, moved)
            value = grad * dsilu[r, :, here]
            zgrad[r, :, here] = value
            u_sum = u_sum + value * norm[r + 1, :, here]
            v_sum = v_sum + value
    uv[0:8] = row_sums(u_sum)
    uv[8:16] = row_sums(v_sum)
    uv_cp = [remote(uv, uv_in.at[d], uv_sem.at[d], {"fsdp": peers_z[d]}) for d in range(nz - 1)]
    for cp in uv_cp:
        cp.start()

    value = quarter[nz - 1].astype(f32)
    for n in range(nz - 1):
        z_cp[n].wait_recv()
    for d in range(nz - 1):
        value = value + z_in[d].astype(f32)
    final[...] = (value * scale).astype(bf16)
    rep_cp = [remote(final, rep_in.at[m], rep_sem.at[m], {"rep": reps[m]}) for m in range(2)]
    for cp in rep_cp:
        cp.start()

    for cp in uv_cp:
        cp.wait_recv()
    total = uv[...]
    for d in range(nz - 1):
        total = total + uv_in[d]
    uvt[...] = total
    uvt_cp = [remote(uvt, uvt_in.at[m], uvt_sem.at[m], {"rep": reps[m]}) for m in range(3)]
    for cp in uvt_cp:
        cp.start()
    grp = dot(same, g_ref[0:1] * total, ((1,), (1,)), HIGHEST)
    su_val = jnp.broadcast_to(grp[:, 0:1] / count, (chans, cols))
    sv_val = jnp.broadcast_to(grp[:, 8:9] / count, (chans, cols))
    rep_cp[1].wait_recv()
    rep_cp.append(remote(rep_in.at[1], rep_in.at[2], rep_sem.at[2], {"rep": core_peer}))
    rep_cp[2].start()

    for r in range(rows):
        for odd in range(2):
            here = pl.ds(odd * cols, cols)
            value = rstd * (gain * zgrad[r, :, here] - sv_val - norm[r + 1, :, here] * su_val)
            patches[r * chans : (r + 1) * chans, here] = value.astype(bf16)
        dx_ref[0, r] = dot(patches[r * chans : (r + 1) * chans], merge).astype(bf16)

    def place(ref, k):
        wg_ref[pl.ds(aligned(q_rows * k), q_rows)] = ref[...].astype(f32)

    place(final, mine)
    for cp in uvt_cp:
        cp.wait_recv()
    total = uvt[...] + uvt_in[0] + uvt_in[1] + uvt_in[2]
    gg_ref[0:1] = total[0:1] * scale
    gg_ref[1:2] = total[8:9] * scale
    owners = [2 * (1 - ci) + xi, 2 * ci + 1 - xi, 2 * (1 - ci) + 1 - xi]
    for m in range(3):
        if m != 1:
            rep_cp[m].wait_recv()
        place(rep_in.at[m], owners[m])

    @pl.when(z < nz - 1)
    def _():
        halo_x.wait_send()

    @pl.when(z > 0)
    def _():
        halo_c.wait_send()

    for group in (
        stat_cp, w_cp, core_cp, fwd_y, fwd_c, fwd_d, x_cp, uv_cp, z_cp, uvt_cp, rep_cp
    ):
        for cp in group:
            cp.wait_send()


def fused_shards(images, gains, conv_weight, cotangent):
    batch, rows, width, chans = images.shape
    block, outs_ch = conv_weight.shape
    if (batch, rows, cotangent.shape[1]) != (1, 4, 2) or block % 16 or outs_ch % 64:
        return shards(images, gains, conv_weight, cotangent)
    nz = lax.axis_size("fsdp")
    cols = width // 2
    q_rows = outs_ch // 4
    f32, bf16 = jnp.float32, jnp.bfloat16
    vmem = pltpu.VMEM
    dma = pltpu.SemaphoreType.DMA
    output_maps, input_grad, weight_grad, gain_grad = pl.pallas_call(
        functools.partial(fused, nz),
        out_shape=(
            jax.ShapeDtypeStruct((batch, rows // 2, outs_ch, cols), bf16),
            jax.ShapeDtypeStruct((batch, rows, chans, width), bf16),
            jax.ShapeDtypeStruct((outs_ch, block), f32),
            jax.ShapeDtypeStruct(gains.shape, f32),
        ),
        in_specs=[pl.BlockSpec(memory_space=vmem)] * 4,
        out_specs=[pl.BlockSpec(memory_space=vmem)] * 4,
        scratch_shapes=[
            vmem((chans, width), bf16),
            vmem((outs_ch, cols), bf16),
            vmem((rows + 1, chans, width), f32),
            vmem((rows, chans, width), f32),
            vmem((rows, chans, width), f32),
            vmem((nz * block, width), bf16),
            vmem((outs_ch, width), bf16),
            vmem((nz * block, width), f32),
            vmem((3 * chans, cols), f32),
            vmem((nz, outs_ch, block), bf16),
            vmem((16, chans), f32),
            vmem((nz - 1, 16, chans), f32),
            vmem((nz, outs_ch, block), bf16),
            vmem((nz, 2 * q_rows, block), bf16),
            vmem((nz, 2 * q_rows, block), bf16),
            vmem((nz, q_rows, block), bf16),
            vmem((nz, q_rows, block), bf16),
            vmem((nz - 1, q_rows, block), bf16),
            vmem((q_rows, block), bf16),
            vmem((3, q_rows, block), bf16),
            vmem((16, chans), f32),
            vmem((nz - 1, 16, chans), f32),
            vmem((16, chans), f32),
            vmem((3, 16, chans), f32),
            dma((2, 2)),
            dma((nz - 1, 2)),
            dma((4, nz - 1, 2)),
            dma((nz, 2)),
            dma((nz, 2)),
            dma((nz - 1, 2)),
            dma((3, 2)),
            dma((nz - 1, 2)),
            dma((3, 2)),
            dma((1,)),
        ],
        compiler_params=pltpu.CompilerParams(
            collective_id=0, has_side_effects=True, vmem_limit_bytes=48 * 1024 * 1024
        ),
    )(
        jnp.swapaxes(images, 2, 3),
        gains,
        conv_weight.T,
        jnp.swapaxes(cotangent, 2, 3),
    )
    return (
        jnp.swapaxes(output_maps, 2, 3),
        jnp.swapaxes(input_grad, 2, 3),
        weight_grad.T,
        gain_grad,
    )


def solution(mesh):
    in_specs = (
        P(("groups", "rep"), "fsdp", None, None),
        P(),
        P("fsdp", None),
        P(("groups", "rep"), "fsdp", None, None),
    )
    out_specs = (
        P(("groups", "rep"), "fsdp", None, None),
        P(("groups", "rep"), "fsdp", None, None),
        P(("groups", "fsdp"), None),
        P("groups", None),
    )
    small = mesh.shape["groups"] == 2 and mesh.shape["rep"] == 4 and mesh.shape["fsdp"] == 4
    body = fused_shards if small else shards
    return jax.shard_map(body, mesh=mesh, in_specs=in_specs, out_specs=out_specs, check_vma=False)
```
